512 devices in a mesh: view: 4 (over x), space: 128 (over y, z, core).
Axes of the slice: x: 4, y: 8, z: 8, core: 2. Of those that a mesh axis runs over, the one named last changes fastest.
Arguments:
- params: float32 [59, 131072], P(None, 'space'), may hold values from -6.5 to 4, as said below
- adam_m: float32 [59, 131072], P(None, 'space'), may hold values from -6 to 6
- adam_v: float32 [59, 131072], P(None, 'space'), may hold values from 0.1 to 10
- visible: int32 [131072], P('space'), may hold values 0 or 1
- cameras: float32 [4, 12], P('view'), may hold values from -1 to 3.2, as said below
- send_index: int32 [4, 128, 512], P('view', 'space'), may hold values from 0 to 1023, as said below
- send_count: int32 [4, 128, 128], P('view', 'space'), may hold values from 0 to 4, as said below
- tile_lists: int32 [4, 256, 512], P('view', 'space'), may hold values from -1 to 511, as said below
- tile_pos: int32 [4, 256], P('view', 'space'), may hold values from 0 to 255, as said below
- target: float32 [4, 5, 65536], P('view', None, 'space'), may hold values from -6 to 6
Outputs:
- image: float32 [4, 5, 65536], P('view', None, 'space')
- new_params: float32 [59, 131072], P(None, 'space')
- new_m: float32 [59, 131072], P(None, 'space')
- new_v: float32 [59, 131072], P(None, 'space')
The draws below stay inside these ranges and needn't reach their ends.
Inputs may be any that keep to these rules, and one draw needn't show every extreme that they name: `params`: centre coordinates within [-2.5, 2.5], every centre at depth 1.5 to 4.5 in front of every camera; log scales within [-6.5, -4.5]; quaternion w within [1, 2] and x, y, z within [-1, 1]; opacity logits within [-4, 4]; harmonic coefficients within [-0.9, 0.9]. `cameras`: a rotation by at most 0.1 radians about each axis, and a translation within 0.2 of (0, 0, 3). `send_index`: the slots of one view, source and destination hold distinct local Gaussian numbers; the slots in use of one source name distinct Gaussians over all views and destinations. `send_count`: in every view some destination device receives 4 slots in use from every source. `tile_lists`: entries of a tile name slots in use towards the tile's device; live entries come first and -1 fills the rest; a slot is named by at most one entry of its view; in every view some tile has 512 entries. `tile_pos`: in each view a permutation of the image's tiles.
All inputs are finite; a program needn't handle non-finite values. No bound on the sum of `visible` on one device may be relied on, other than what follows from the above.
Results may differ from the reference program's by a relative error of at most 0.0003.
Values sent between devices are 32-bit elements; how exact they have to be, the bound alone decides.
No kernel may reach another device: no remote copies, remote signals or barrier semaphores. Data moves between devices by JAX's collectives and lax.ppermute only.
A program may use at most 64 MiB of HBM per device.

```python
import math
import jax
import jax.numpy as jnp
from jax import lax

NPARAM = 59
LIST = 512
G_DEV = 1024
TILE_DEV = 2
CAP = 4
NVIEW = 4
G = 131072
TILES_VIEW = 256
PIX = 65536


def camera_table(key):
    angles = jax.random.uniform(jax.random.fold_in(key, 3), (NVIEW, 3), jnp.float32, -0.1, 0.1)
    moved = jax.random.uniform(jax.random.fold_in(key, 5), (NVIEW, 3), jnp.float32, -0.2, 0.2)
    cosine = jnp.cos(angles)
    sine = jnp.sin(angles)
    zeros = jnp.zeros((NVIEW,), jnp.float32)
    ones = jnp.ones((NVIEW,), jnp.float32)
    turn_x = jnp.stack([ones, zeros, zeros, zeros, cosine[:, 0], -sine[:, 0], zeros, sine[:, 0], cosine[:, 0]], 1).reshape(NVIEW, 3, 3)
    turn_y = jnp.stack([cosine[:, 1], zeros, sine[:, 1], zeros, ones, zeros, -sine[:, 1], zeros, cosine[:, 1]], 1).reshape(NVIEW, 3, 3)
    turn_z = jnp.stack([cosine[:, 2], -sine[:, 2], zeros, sine[:, 2], cosine[:, 2], zeros, zeros, zeros, ones], 1).reshape(NVIEW, 3, 3)
    whole = jnp.einsum('nij,njk->nik', jnp.einsum('nij,njk->nik', turn_z, turn_y), turn_x)
    offset = moved + jnp.array([0.0, 0.0, 3.0], jnp.float32)[None, :]
    return jnp.concatenate([whole.reshape(NVIEW, 9), offset], axis=1)


def routing_counts(key):
    shards = G // G_DEV
    block_size = G_DEV // NVIEW
    spare = block_size - CAP
    keys = jax.random.split(jax.random.fold_in(key, 7), 2)
    full_dest = jax.random.randint(keys[0], (NVIEW,), 0, shards)
    targets = jax.random.randint(keys[1], (NVIEW, shards, spare), 0, shards)
    view_idx = jnp.broadcast_to(jnp.arange(NVIEW, dtype=jnp.int32)[:, None, None], targets.shape)
    source_idx = jnp.broadcast_to(jnp.arange(shards, dtype=jnp.int32)[None, :, None], targets.shape)
    tallies = jnp.zeros((NVIEW, shards, shards), jnp.int32).at[view_idx, source_idx, targets].add(1)
    counts = jnp.minimum(tallies, CAP)
    places = jnp.arange(shards, dtype=jnp.int32)[None, None, :]
    counts = jnp.where(places == full_dest[:, None, None], CAP, counts)
    return (counts.astype(jnp.int32), full_dest)


def routing_index(key):
    counts, full_dest = routing_counts(key)
    shards = G // G_DEV
    block_size = G_DEV // NVIEW
    orders = jax.vmap(lambda inner: jax.random.permutation(inner, G_DEV))(jax.random.split(jax.random.fold_in(key, 13), shards))
    starts = jnp.cumsum(counts, axis=2) - counts
    slot_ids = jnp.arange(CAP, dtype=jnp.int32)[None, None, None, :]
    view_ids = jnp.arange(NVIEW, dtype=jnp.int32)[:, None, None, None]
    position = (view_ids * block_size + starts[..., None] + slot_ids) % G_DEV
    source_ids = jnp.broadcast_to(jnp.arange(shards, dtype=jnp.int32)[None, :, None, None], position.shape)
    local = orders[source_ids, position]
    return local.reshape(NVIEW, shards, shards * CAP).astype(jnp.int32)


def tile_places(key):
    keys = jax.random.split(jax.random.fold_in(key, 17), NVIEW)
    return jax.vmap(lambda inner: jax.random.permutation(inner, TILES_VIEW))(keys).astype(jnp.int32)


def list_table(key):
    counts, full_dest = routing_counts(key)
    shards = G // G_DEV
    slot_total = shards * CAP
    keys = jax.random.split(jax.random.fold_in(key, 11), 4)
    entry = jnp.arange(slot_total, dtype=jnp.int32)
    source = entry // CAP
    slot = entry % CAP
    live = slot[None, None, :] < jnp.transpose(counts[:, source, :], (0, 2, 1))
    home = jax.random.randint(keys[0], (NVIEW, shards, slot_total), 0, TILE_DEV)
    ranking = jax.vmap(lambda inner: jax.random.permutation(inner, slot_total))(jax.random.split(keys[1], NVIEW))
    full_tile = jax.random.randint(keys[2], (NVIEW,), 0, TILE_DEV)
    at_full = jnp.arange(shards, dtype=jnp.int32)[None, :, None] == full_dest[:, None, None]
    home = jnp.where(at_full & (ranking[:, None, :] < LIST), full_tile[:, None, None], home)
    ordering = jax.vmap(lambda inner: jax.random.permutation(inner, slot_total))(jax.random.split(keys[3], NVIEW * shards)).reshape(NVIEW, shards, slot_total)
    tile_ids = jnp.arange(TILE_DEV, dtype=jnp.int32)[None, None, :, None]
    member = live[:, :, None, :] & (home[:, :, None, :] == tile_ids)
    scores = jnp.where(member, ordering[:, :, None, :], slot_total + entry[None, None, None, :])
    picked = jnp.argsort(scores, axis=3)[..., :LIST]
    kept = jnp.take_along_axis(scores, picked, axis=3) < slot_total
    lists = jnp.where(kept, picked, -1)
    return lists.reshape(NVIEW, TILES_VIEW, LIST).astype(jnp.int32)


def draw_cameras(key, part):
    return camera_table(key)


def draw_send_count(key, part):
    return routing_counts(key)[0]


def draw_send_index(key, part):
    return routing_index(key)


def draw_tile_lists(key, part):
    return list_table(key)


def draw_tile_pos(key, part):
    return tile_places(key)


def draw_params(key, part):
    own = jax.random.split(jax.random.fold_in(key, 23), 9)
    lists = list_table(key)
    index = routing_index(key)
    places = tile_places(key)
    cameras = camera_table(key)
    live = lists >= 0
    clipped = jnp.maximum(lists, 0)
    source = clipped // CAP
    owner = (jnp.arange(TILES_VIEW, dtype=jnp.int32) // TILE_DEV)[None, :, None]
    view_ids = jnp.arange(NVIEW, dtype=jnp.int32)[:, None, None]
    local = index[view_ids, source, owner * CAP + clipped % CAP]
    gauss_ids = jnp.where(live, source * G_DEV + local, G)
    tiles = places[:, :, None]
    shape = (NVIEW, TILES_VIEW, LIST)
    pixel_x = (16 * (tiles % 64)).astype(jnp.float32) + jax.random.uniform(own[0], shape, jnp.float32, 0.5, 15.5)
    pixel_y = (16 * (tiles // 64)).astype(jnp.float32) + jax.random.uniform(own[1], shape, jnp.float32, 0.5, 15.5)
    steps = jnp.arange(LIST, dtype=jnp.float32)[None, None, :]
    depth = 2.7 + 0.6 * (steps + jax.random.uniform(own[2], shape, jnp.float32, 0.1, 0.9)) / LIST
    center_y = 8.0 * TILES_VIEW / 64.0
    camera_pts = jnp.stack([(pixel_x - 512.0) * depth / 1000.0, (pixel_y - center_y) * depth / 1000.0, depth])
    rotation = cameras[:, :9].reshape(NVIEW, 3, 3)
    offset = jnp.transpose(cameras[:, 9:12])[:, :, None, None]
    world = jnp.einsum('wrc,rwtl->cwtl', rotation, camera_pts - offset)
    low = jnp.array([-1.5, -0.4, -0.4], jnp.float32)[:, None]
    high = jnp.array([1.5, 0.4, 0.4], jnp.float32)[:, None]
    centre = low + (high - low) * jax.random.uniform(own[3], (3, G), jnp.float32)
    centre = centre.at[:, gauss_ids.reshape(-1)].set(world.reshape(3, -1), mode='drop')
    log_scales = jax.random.uniform(own[4], (3, G), jnp.float32, -6.5, -4.5)
    quat_w = jax.random.uniform(own[5], (1, G), jnp.float32, 1.0, 2.0)
    quat_rest = jax.random.uniform(own[6], (3, G), jnp.float32, -1.0, 1.0)
    logits = jax.random.uniform(own[7], (1, G), jnp.float32, -4.0, 4.0)
    harmonics = jnp.clip(0.3 * jax.random.normal(own[8], (48, G), jnp.float32), -0.9, 0.9)
    return jnp.concatenate([centre, log_scales, quat_w, quat_rest, logits, harmonics], axis=0)


def with_ends(values, key, smallest, high):
    longest = values.shape.index(max(values.shape))
    spots = []
    for shift in (0, 1):
        where = [jax.random.randint(jax.random.fold_in(key, axis), (), 0, length) for axis, length in enumerate(values.shape)]
        where[longest] = (where[longest] + shift) % values.shape[longest]
        spots.append(tuple(where))
    return values.at[spots[0]].set(smallest).at[spots[1]].set(high)


def block_scale(rng, dims, cuts, least, top_value):
    loudness, own = 1.0, jax.random.fold_in(rng, 6)
    for dim, shards_of in cuts:
        draws = jnp.exp(jax.random.uniform(jax.random.fold_in(own, dim), (shards_of,), jnp.float32, least / len(cuts), top_value / len(cuts)))
        loudness = loudness * jnp.repeat(draws, dims[dim] // shards_of).reshape([-1 if axis == dim else 1 for axis in range(len(dims))])
    return loudness


def noise(key, dims, width, most, pieces=(), kind=jnp.bfloat16):
    values = width * jax.random.normal(key, dims, jnp.float32)
    if pieces:
        values = values * block_scale(key, dims, pieces, -0.22, 0.18)
    return jnp.clip(values, -most, most).astype(kind)


def setup_inputs(seed: int = 0) -> dict:
    splits = jax.random.split(jax.random.key(seed), 11)
    return {
        "params": draw_params(jax.random.fold_in(splits[10], 71), 0),
        "adam_m": noise(splits[1], (NPARAM, G), 1.0, 6.0, ((1, 128),), jnp.float32),
        "adam_v": jnp.clip(jnp.exp(math.log(10.0) - 4.6051702 * jax.random.uniform(splits[2], (NPARAM, G), jnp.float32) ** block_scale(splits[2], (NPARAM, G), ((1, 128),), -0.2, 0.2)), 0.1, 10.0),
        "visible": with_ends((jax.random.randint(splits[3], (G,), 0, 4) < 3).astype(jnp.int32), jax.random.fold_in(splits[3], 1), 0, 1),
        "cameras": draw_cameras(jax.random.fold_in(splits[10], 71), 0),
        "send_index": draw_send_index(jax.random.fold_in(splits[10], 71), 0),
        "send_count": draw_send_count(jax.random.fold_in(splits[10], 71), 0),
        "tile_lists": draw_tile_lists(jax.random.fold_in(splits[10], 71), 0),
        "tile_pos": draw_tile_pos(jax.random.fold_in(splits[10], 71), 0),
        "target": noise(splits[9], (NVIEW, 5, PIX), 1.0, 6.0, ((0, 4), (2, 128)), jnp.float32),
    }


focal_len = 1000.0
center_x = 512.0
harm_zero = 0.28209479177387814
harm_one = 0.4886025119029199
harm_two = (1.0925484305920792, -1.0925484305920792, 0.31539156525252005, -1.0925484305920792, 0.5462742152960396)
harm_three = (-0.5900435899266435, 2.890611442640554, -0.4570457994644658, 0.3731763325901154, -0.4570457994644658, 1.445305721320277, -0.5900435899266435)
beta_one = 0.9
beta_two = 0.99
learn_rate = 0.05
adam_eps = 1e-08
adam_step = 100.0

def project(gauss, camera, center_y):
    rotation = [[camera[3 * i + j] for j in range(3)] for i in range(3)]
    offset = [camera[9 + i] for i in range(3)]
    centre = [gauss[i] for i in range(3)]
    viewed = [sum((rotation[i][j] * centre[j] for j in range(3))) + offset[i] for i in range(3)]
    inverse = 1.0 / viewed[2]
    screen_x = focal_len * viewed[0] * inverse + center_x
    screen_y = focal_len * viewed[1] * inverse + center_y
    scales = [jnp.exp(gauss[3 + i]) for i in range(3)]
    length = jnp.sqrt(gauss[6] * gauss[6] + gauss[7] * gauss[7] + gauss[8] * gauss[8] + gauss[9] * gauss[9])
    quat_w, quat_x, quat_y, quat_z = [gauss[6 + i] / length for i in range(4)]
    spin = [[1.0 - 2.0 * (quat_y * quat_y + quat_z * quat_z), 2.0 * (quat_x * quat_y - quat_w * quat_z), 2.0 * (quat_x * quat_z + quat_w * quat_y)], [2.0 * (quat_x * quat_y + quat_w * quat_z), 1.0 - 2.0 * (quat_x * quat_x + quat_z * quat_z), 2.0 * (quat_y * quat_z - quat_w * quat_x)], [2.0 * (quat_x * quat_z - quat_w * quat_y), 2.0 * (quat_y * quat_z + quat_w * quat_x), 1.0 - 2.0 * (quat_x * quat_x + quat_y * quat_y)]]
    factor = [[spin[i][j] * scales[j] for j in range(3)] for i in range(3)]
    sigma = [[sum((factor[i][j] * factor[k][j] for j in range(3))) for k in range(3)] for i in range(3)]
    near = focal_len * inverse
    lean_x = -focal_len * viewed[0] * inverse * inverse
    lean_y = -focal_len * viewed[1] * inverse * inverse
    jacob = [[near * rotation[0][j] + lean_x * rotation[2][j] for j in range(3)], [near * rotation[1][j] + lean_y * rotation[2][j] for j in range(3)]]
    halfway = [[sum((jacob[a][i] * sigma[i][k] for i in range(3))) for k in range(3)] for a in range(2)]
    upper = sum((halfway[0][k] * jacob[0][k] for k in range(3))) + 0.3
    middle = sum((halfway[0][k] * jacob[1][k] for k in range(3)))
    lower = sum((halfway[1][k] * jacob[1][k] for k in range(3))) + 0.3
    determinant = upper * lower - middle * middle
    conic_a = lower / determinant
    conic_b = -middle / determinant
    conic_c = upper / determinant
    opacity = jax.nn.sigmoid(gauss[10])
    camera_pos = [-sum((rotation[i][j] * offset[i] for i in range(3))) for j in range(3)]
    toward = [centre[j] - camera_pos[j] for j in range(3)]
    reach = jnp.sqrt(toward[0] * toward[0] + toward[1] * toward[1] + toward[2] * toward[2])
    unit_x = toward[0] / reach
    unit_y = toward[1] / reach
    unit_z = toward[2] / reach
    square_x = unit_x * unit_x
    square_y = unit_y * unit_y
    square_z = unit_z * unit_z
    basis = [harm_zero + 0.0 * unit_x, -harm_one * unit_y, harm_one * unit_z, -harm_one * unit_x, harm_two[0] * unit_x * unit_y, harm_two[1] * unit_y * unit_z, harm_two[2] * (2.0 * square_z - square_x - square_y), harm_two[3] * unit_x * unit_z, harm_two[4] * (square_x - square_y), harm_three[0] * unit_y * (3.0 * square_x - square_y), harm_three[1] * unit_x * unit_y * unit_z, harm_three[2] * unit_y * (4.0 * square_z - square_x - square_y), harm_three[3] * unit_z * (2.0 * square_z - 3.0 * square_x - 3.0 * square_y), harm_three[4] * unit_x * (4.0 * square_z - square_x - square_y), harm_three[5] * unit_z * (square_x - square_y), harm_three[6] * unit_x * (square_x - 3.0 * square_y)]
    colors = [0.5 + sum((basis[k] * gauss[11 + 16 * c + k] for k in range(16))) for c in range(3)]
    return jnp.stack([screen_x, screen_y, conic_a, conic_b, conic_c, opacity, colors[0], colors[1], colors[2], viewed[2], inverse])

def shade_tile(entries, valid, tile):
    lane = jnp.arange(256, dtype=jnp.int32)
    column = tile % 64 * 16 + lane % 16
    height = tile // 64 * 16 + lane // 16
    pixel_x = column.astype(entries.dtype) + 0.5
    pixel_y = height.astype(entries.dtype) + 0.5
    apart_x = pixel_x[:, None] - entries[0][None, :]
    apart_y = pixel_y[:, None] - entries[1][None, :]
    quad = entries[2][None, :] * apart_x * apart_x + 2.0 * entries[3][None, :] * apart_x * apart_y + entries[4][None, :] * apart_y * apart_y
    alpha = entries[5][None, :] * jnp.exp(-0.5 * quad) * valid[None, :]
    keeping = jnp.log1p(-alpha)
    weight = alpha * jnp.exp(jnp.cumsum(keeping, axis=1) - keeping)
    feats = entries[6:11]
    return lax.dot_general(feats, weight, (((1,), (1,)), ((), ())), precision=lax.Precision.HIGHEST)

def adam_update(params, adam_m, adam_v, grad, visible):
    moment_one = beta_one * adam_m + (1.0 - beta_one) * grad
    moment_two = beta_two * adam_v + (1.0 - beta_two) * grad * grad
    first_hat = moment_one / (1.0 - beta_one ** adam_step)
    second_hat = moment_two / (1.0 - beta_two ** adam_step)
    stepped = params - learn_rate * first_hat / (jnp.sqrt(second_hat) + adam_eps)
    keep = (visible > 0)[None, :]
    return (jnp.where(keep, stepped, params), jnp.where(keep, moment_one, adam_m), jnp.where(keep, moment_two, adam_v))

def reference(params, adam_m, adam_v, visible, cameras, send_index, send_count, tile_lists, tile_pos, target):
    center_y = 8.0 * TILES_VIEW / 64.0
    owner = jnp.arange(TILES_VIEW, dtype=jnp.int32) // TILE_DEV

    def render(gauss):
        images = []
        for view in range(NVIEW):
            records = project(gauss, cameras[view], center_y)
            lists = tile_lists[view]
            live = lists >= 0
            clipped = jnp.maximum(lists, 0).astype(jnp.int32)
            source = clipped // CAP
            slot = clipped % CAP
            limit = send_count[view][source, owner[:, None]]
            valid = live & (slot < limit)
            local = send_index[view][source, owner[:, None] * CAP + slot]
            global_ids = (source * G_DEV + local).astype(jnp.int32)

            def one_tile(item):
                gauss_ids, usable, tile = item
                return shade_tile(records[:, gauss_ids], usable.astype(records.dtype), tile)
            tiles = lax.map(jax.checkpoint(one_tile), (global_ids, valid, tile_pos[view]))
            images.append(jnp.transpose(tiles, (1, 0, 2)).reshape(5, PIX))
        return jnp.stack(images)
    image, pullback = jax.vjp(render, params)
    grad, = pullback(image - target)
    new_params, new_m, new_v = adam_update(params, adam_m, adam_v, grad, visible)
    return (image, new_params, new_m, new_v)
```

```python
import functools

import jax
import jax.numpy as jnp
from jax import lax
from jax.experimental import pallas as pl
from jax.experimental.pallas import tpu as pltpu
from jax.sharding import PartitionSpec as P

focal_len = 1000.0
center_x = 512.0
harm_zero = 0.28209479177387814
harm_one = 0.4886025119029199
harm_two = (
    1.0925484305920792,
    -1.0925484305920792,
    0.31539156525252005,
    -1.0925484305920792,
    0.5462742152960396,
)
harm_three = (
    -0.5900435899266435,
    2.890611442640554,
    -0.4570457994644658,
    0.3731763325901154,
    -0.4570457994644658,
    1.445305721320277,
    -0.5900435899266435,
)
beta_one = 0.9
beta_two = 0.99
learn_rate = 0.05
adam_eps = 1e-08
adam_step = 100.0
num_param = 59
num_record = 11
num_view = 4
gauss_dev = 1024
shards = 128
cap = 4
slots = 512
slot_rows = 16
tile_dev = 2
list_len = 512


def project(gauss, camera, center_y):
    rotation = [[camera[3 * i + j] for j in range(3)] for i in range(3)]
    offset = [camera[9 + i] for i in range(3)]
    centre = [gauss[i] for i in range(3)]
    viewed = [sum((rotation[i][j] * centre[j] for j in range(3))) + offset[i] for i in range(3)]
    inverse = 1.0 / viewed[2]
    screen_x = focal_len * viewed[0] * inverse + center_x
    screen_y = focal_len * viewed[1] * inverse + center_y
    scales = [jnp.exp(gauss[3 + i]) for i in range(3)]
    length = jnp.sqrt(
        gauss[6] * gauss[6] + gauss[7] * gauss[7] + gauss[8] * gauss[8] + gauss[9] * gauss[9]
    )
    quat_w, quat_x, quat_y, quat_z = [gauss[6 + i] / length for i in range(4)]
    spin = [
        [
            1.0 - 2.0 * (quat_y * quat_y + quat_z * quat_z),
            2.0 * (quat_x * quat_y - quat_w * quat_z),
            2.0 * (quat_x * quat_z + quat_w * quat_y),
        ],
        [
            2.0 * (quat_x * quat_y + quat_w * quat_z),
            1.0 - 2.0 * (quat_x * quat_x + quat_z * quat_z),
            2.0 * (quat_y * quat_z - quat_w * quat_x),
        ],
        [
            2.0 * (quat_x * quat_z - quat_w * quat_y),
            2.0 * (quat_y * quat_z + quat_w * quat_x),
            1.0 - 2.0 * (quat_x * quat_x + quat_y * quat_y),
        ],
    ]
    factor = [[spin[i][j] * scales[j] for j in range(3)] for i in range(3)]
    sigma = [
        [sum((factor[i][j] * factor[k][j] for j in range(3))) for k in range(3)] for i in range(3)
    ]
    near = focal_len * inverse
    lean_x = -focal_len * viewed[0] * inverse * inverse
    lean_y = -focal_len * viewed[1] * inverse * inverse
    jacob = [
        [near * rotation[0][j] + lean_x * rotation[2][j] for j in range(3)],
        [near * rotation[1][j] + lean_y * rotation[2][j] for j in range(3)],
    ]
    halfway = [
        [sum((jacob[a][i] * sigma[i][k] for i in range(3))) for k in range(3)] for a in range(2)
    ]
    upper = sum((halfway[0][k] * jacob[0][k] for k in range(3))) + 0.3
    middle = sum((halfway[0][k] * jacob[1][k] for k in range(3)))
    lower = sum((halfway[1][k] * jacob[1][k] for k in range(3))) + 0.3
    determinant = upper * lower - middle * middle
    conic_a = lower / determinant
    conic_b = -middle / determinant
    conic_c = upper / determinant
    opacity = jax.nn.sigmoid(gauss[10])
    camera_pos = [-sum((rotation[i][j] * offset[i] for i in range(3))) for j in range(3)]
    toward = [centre[j] - camera_pos[j] for j in range(3)]
    reach = jnp.sqrt(toward[0] * toward[0] + toward[1] * toward[1] + toward[2] * toward[2])
    unit_x = toward[0] / reach
    unit_y = toward[1] / reach
    unit_z = toward[2] / reach
    square_x = unit_x * unit_x
    square_y = unit_y * unit_y
    square_z = unit_z * unit_z
    basis = [
        harm_zero + 0.0 * unit_x,
        -harm_one * unit_y,
        harm_one * unit_z,
        -harm_one * unit_x,
        harm_two[0] * unit_x * unit_y,
        harm_two[1] * unit_y * unit_z,
        harm_two[2] * (2.0 * square_z - square_x - square_y),
        harm_two[3] * unit_x * unit_z,
        harm_two[4] * (square_x - square_y),
        harm_three[0] * unit_y * (3.0 * square_x - square_y),
        harm_three[1] * unit_x * unit_y * unit_z,
        harm_three[2] * unit_y * (4.0 * square_z - square_x - square_y),
        harm_three[3] * unit_z * (2.0 * square_z - 3.0 * square_x - 3.0 * square_y),
        harm_three[4] * unit_x * (4.0 * square_z - square_x - square_y),
        harm_three[5] * unit_z * (square_x - square_y),
        harm_three[6] * unit_x * (square_x - 3.0 * square_y),
    ]
    colors = [0.5 + sum((basis[k] * gauss[11 + 16 * c + k] for k in range(16))) for c in range(3)]
    return [
        screen_x,
        screen_y,
        conic_a,
        conic_b,
        conic_c,
        opacity,
        colors[0],
        colors[1],
        colors[2],
        viewed[2],
        inverse,
    ]


def split_three(values):
    high = values.astype(jnp.bfloat16)
    left = values - high.astype(jnp.float32)
    middle = left.astype(jnp.bfloat16)
    low = (left - middle.astype(jnp.float32)).astype(jnp.bfloat16)
    return high, middle, low


def contract(left, right, left_dim, right_dim):
    return lax.dot_general(
        left,
        right,
        (((left_dim,), (right_dim,)), ((), ())),
        preferred_element_type=jnp.float32,
    )


def as_mask(condition):
    return jnp.where(condition, 1.0, 0.0).astype(jnp.bfloat16)


def gather_exact(rows, choose, choose_dim):
    count = rows.shape[0]
    out = contract(jnp.concatenate(split_three(rows), axis=0), choose, 1, choose_dim)
    return out[:count] + (out[count : 2 * count] + out[2 * count :])


def send_kernel(center_y, params, route, count, camera, out, turned):
    rows = params[...].reshape(num_param, 8, 128)
    cam = [camera[0, i] for i in range(12)]
    records = project([rows[i] for i in range(num_param)], cam, center_y)
    records = records + [jnp.zeros_like(records[0])] * (slot_rows - num_record)
    table = jnp.stack(records).reshape(slot_rows, gauss_dev)
    chosen = route[0]
    local = lax.broadcasted_iota(jnp.int32, (gauss_dev, slots), 0)
    sent = gather_exact(table, as_mask(local == chosen), 0)
    which = lax.broadcasted_iota(jnp.int32, (slot_rows, slots), 0)
    sent = jnp.where(which == num_record, (chosen + 1).astype(jnp.float32), sent)
    turned[:, 0:slot_rows] = sent.T
    parts = [turned[pl.ds(c, shards, stride=cap), :][:, 0:slot_rows] for c in range(cap)]
    width = cap * slot_rows
    spread = jnp.concatenate(parts + [jnp.zeros((shards, 128 - width), jnp.float32)], axis=1)
    used = jnp.broadcast_to(count[0], (8, shards)).T[:, 0:1]
    lane = lax.broadcasted_iota(jnp.int32, (shards, 128), 1)
    out[...] = jnp.where(lane // slot_rows < used, spread, 0.0)


def tile_kernel(arrived, lists, places, target, image, out):
    turned = arrived[...].T
    rec = jnp.concatenate([turned[c * slot_rows : (c + 1) * slot_rows] for c in range(cap)], axis=1)
    order = jnp.concatenate([lists[0, t : t + 1] for t in range(tile_dev)], axis=1)
    total = tile_dev * list_len
    spot = lax.broadcasted_iota(jnp.int32, (slots, total), 0)
    slot_id = cap * (spot % shards) + spot // shards
    found = as_mask(slot_id == order)
    number = lax.broadcasted_iota(jnp.int32, (8, total), 1) + 1
    digit = lax.broadcasted_iota(jnp.int32, (8, total), 0)
    digits = jnp.where(digit == 0, number // 256, number % 256).astype(jnp.float32)
    keys = contract(digits.astype(jnp.bfloat16), found, 1, 1)
    key = 256.0 * keys[0:1] + keys[1:2]
    key_col = jnp.broadcast_to(key, (8, slots)).T[:, 0:1]
    second = key > float(list_len)
    floor = jnp.where(second, float(list_len), 0.0)
    before = as_mask((key_col < key) & (key_col > floor))
    corner_x = [(places[0, t] % 64 * 16).astype(jnp.float32) + 8.0 for t in range(tile_dev)]
    corner_y = [(places[0, t] // 64 * 16).astype(jnp.float32) + 8.0 for t in range(tile_dev)]
    at_x = rec[0:1] - jnp.where(second, corner_x[1], corner_x[0])
    at_y = rec[1:2] - jnp.where(second, corner_y[1], corner_y[0])
    con_a, con_b, con_c = rec[2:3], rec[3:4], rec[4:5]
    opacity = jnp.where(key > 0.0, rec[5:6], 0.0)
    lane = lax.broadcasted_iota(jnp.int32, (256, 1), 0)
    pix_x = (lane % 16).astype(jnp.float32) - 7.5
    pix_y = (lane // 16).astype(jnp.float32) - 7.5
    apart_x = pix_x - at_x
    apart_y = pix_y - at_y
    half_a, half_c = -0.5 * con_a, -0.5 * con_c
    power = apart_x * (half_a * apart_x - con_b * apart_y) + half_c * apart_y * apart_y
    alpha = opacity * jnp.exp(power)
    keep = 1.0 - alpha
    logs = jnp.concatenate(split_three(jnp.log(keep)), axis=0)
    sums = contract(logs, before, 1, 0)
    through = jnp.exp(sums[0:256] + (sums[256:512] + sums[512:768]))
    weight = alpha * through
    w_hi, w_mid, w_lo = split_three(weight)
    feats = rec[6:11]
    gap = jnp.zeros((3, slots), jnp.float32)
    feats = jnp.concatenate(
        [jnp.where(second, 0.0, feats), gap, jnp.where(second, feats, 0.0), gap], axis=0
    )
    f_hi, f_mid, f_lo = split_three(feats)
    f_all = jnp.concatenate([f_hi, f_mid, f_lo], axis=0)
    drawn_hi = contract(f_all, w_hi, 1, 1)
    drawn_mid = contract(f_all[0:32], w_mid, 1, 1)
    drawn_lo = contract(f_all[0:16], w_lo, 1, 1)
    drawn = drawn_hi[0:16] + (
        (drawn_hi[16:32] + drawn_mid[0:16]) + (drawn_hi[32:48] + drawn_mid[16:32] + drawn_lo)
    )
    shown = jnp.concatenate([drawn[0:5], drawn[8:13]], axis=1)
    image[0] = shown
    diff = shown - target[0]
    gap = jnp.zeros((3, 256), jnp.float32)
    residue = jnp.concatenate([diff[:, 0:256], gap, diff[:, 256:512], gap], axis=0)
    g_hi, g_mid, g_lo = split_three(residue)
    g_six = jnp.concatenate([g_hi, g_hi, g_mid, g_mid, g_hi, g_lo], axis=0)
    f_six = jnp.concatenate([f_hi, f_mid, f_hi, f_mid, f_lo, f_hi], axis=0)
    score = contract(g_six, f_six, 0, 0)
    tails = contract(jnp.concatenate(split_three(weight * score), axis=0), before, 1, 1)
    tail = tails[0:256] + (tails[256:512] + tails[512:768])
    pull = alpha * (through * score - tail / keep)
    seat = lax.broadcasted_iota(jnp.int32, (8, 256), 1)
    row = lax.broadcasted_iota(jnp.int32, (8, 256), 0)
    seat_x = (seat % 16).astype(jnp.float32) - 7.5
    seat_y = (seat // 16).astype(jnp.float32) - 7.5
    first = jnp.where((row == 1) | (row == 3) | (row == 4), seat_x, 1.0)
    first = jnp.where((row == 2) | (row == 5), seat_y, first)
    other = jnp.where(row == 3, seat_x, 1.0)
    other = jnp.where((row == 4) | (row == 5), seat_y, other)
    basis = (first * other).astype(jnp.bfloat16)
    moments = contract(
        jnp.concatenate([basis] * 3, axis=1), jnp.concatenate(split_three(pull), axis=0), 1, 0
    )
    m_0, m_x, m_y, m_xx, m_xy, m_yy = [moments[i : i + 1] for i in range(6)]
    d_x = m_x - at_x * m_0
    d_y = m_y - at_y * m_0
    d_xx = m_xx - at_x * (m_x + d_x)
    d_xy = m_xy - at_x * m_y - at_y * d_x
    d_yy = m_yy - at_y * (m_y + d_y)
    g_all = jnp.concatenate([g_hi, g_mid, g_lo], axis=0)
    color_hi = contract(g_all, w_hi, 1, 0)
    color_mid = contract(g_all[0:32], w_mid, 1, 0)
    color_lo = contract(g_all[0:16], w_lo, 1, 0)
    color = color_hi[0:16] + (
        (color_hi[16:32] + color_mid[0:16]) + (color_hi[32:48] + color_mid[16:32] + color_lo)
    )
    color = jnp.where(second, color[8:13], color[0:5])
    pulled = jnp.concatenate(
        [
            con_a * d_x + con_b * d_y,
            con_b * d_x + con_c * d_y,
            -0.5 * d_xx,
            -d_xy,
            -0.5 * d_yy,
            jnp.where(opacity > 0.0, m_0 / jnp.where(opacity > 0.0, opacity, 1.0), 0.0),
            color,
            rec[11:12],
            jnp.zeros((4, slots), jnp.float32),
        ],
        axis=0,
    )
    stacked = [pulled[:, c * shards : (c + 1) * shards] for c in range(cap)]
    stacked = jnp.concatenate(stacked + [jnp.zeros((128 - cap * slot_rows, shards))], axis=0)
    out[...] = stacked.T


def place_kernel(returned, camera, out):
    turned = returned[...].T
    rec = jnp.concatenate([turned[c * slot_rows : (c + 1) * slot_rows] for c in range(cap)], axis=1)
    number = rec[11:12]
    local = lax.broadcasted_iota(jnp.int32, (gauss_dev, slots), 0).astype(jnp.float32) + 1.0
    row = lax.broadcasted_iota(jnp.int32, (slot_rows, slots), 0)
    rec = jnp.where(row == num_record, 1.0, rec)
    placed = gather_exact(rec, as_mask(local == number), 1)
    lane = lax.broadcasted_iota(jnp.int32, (1, 128), 1)
    cams = jnp.zeros((1, 128), jnp.float32)
    for i in range(12):
        cams = jnp.where(lane == i, camera[0, i], cams)
    block = placed.reshape(slot_rows, 8, 128)
    for w in range(num_view):
        out[w] = block
        out[w, num_record + 1, 0:1] = cams


def update_kernel(center_y, grads, params, adam_m, adam_v, visible, new_p, new_m, new_v):
    used = [grads[w, num_record] > 0.5 for w in range(num_view)]
    cam = []
    for i in range(12):
        value = jnp.broadcast_to(grads[0, num_record + 1, 0:1, i : i + 1], (8, 128))
        for w in range(1, num_view):
            value = jnp.where(used[w], grads[w, num_record + 1, 0:1, i : i + 1], value)
        cam.append(value)
    pulled = [sum(grads[w, r] for w in range(num_view)) for r in range(num_record)]
    rows = params[...].reshape(num_param, 8, 128)
    _, pull = jax.vjp(
        lambda *gauss: project(gauss, cam, center_y), *[rows[i] for i in range(num_param)]
    )
    grad = jnp.stack(pull(pulled)).reshape(num_param, gauss_dev)
    keep = jnp.broadcast_to(visible[...].reshape(1, gauss_dev) > 0, grad.shape)
    old, old_m, old_v = params[...], adam_m[...], adam_v[...]
    moment_one = beta_one * old_m + (1.0 - beta_one) * grad
    moment_two = beta_two * old_v + (1.0 - beta_two) * grad * grad
    first_hat = moment_one / (1.0 - beta_one**adam_step)
    second_hat = moment_two / (1.0 - beta_two**adam_step)
    stepped = old - learn_rate * first_hat / (jnp.sqrt(second_hat) + adam_eps)
    new_p[...] = jnp.where(keep, stepped, old)
    new_m[...] = jnp.where(keep, moment_one, old_m)
    new_v[...] = jnp.where(keep, moment_two, old_v)


def shaped(*dims):
    return jax.ShapeDtypeStruct(dims, jnp.float32)


vector = pl.BlockSpec(memory_space=pltpu.VMEM)
scalar = pl.BlockSpec(memory_space=pltpu.SMEM)


def send_call(params, send_index, send_count, cameras):
    return pl.pallas_call(
        functools.partial(send_kernel, 8.0 * (tile_dev * shards) / 64.0),
        out_shape=shaped(shards, 128),
        in_specs=[vector, vector, vector, scalar],
        scratch_shapes=[pltpu.VMEM((slots, 128), jnp.float32)],
        name="send",
    )(params, send_index, send_count, cameras)


def tile_call(arrived, tile_lists, tile_pos, target):
    return pl.pallas_call(
        tile_kernel,
        out_shape=(shaped(1, 5, tile_dev * 256), shaped(shards, 128)),
        in_specs=[vector, vector, scalar, vector],
        name="tiles",
    )(arrived, tile_lists, tile_pos, target)


def place_call(returned, cameras):
    return pl.pallas_call(
        place_kernel,
        out_shape=shaped(num_view, slot_rows, 8, 128),
        in_specs=[vector, scalar],
        name="place",
    )(returned, cameras)


def update_call(grads, params, adam_m, adam_v, visible):
    return pl.pallas_call(
        functools.partial(update_kernel, 8.0 * (tile_dev * shards) / 64.0),
        out_shape=(shaped(num_param, gauss_dev),) * 3,
        in_specs=[vector] * 5,
        name="update",
    )(grads, params, adam_m, adam_v, visible)


def body(
    params, adam_m, adam_v, visible, cameras, send_index, send_count, tile_lists, tile_pos, target
):
    sending = send_call(params, send_index, send_count, cameras)
    arrived = lax.all_to_all(sending, "space", split_axis=0, concat_axis=0, tiled=True)
    image, pulled = tile_call(arrived, tile_lists, tile_pos, target)
    returned = lax.all_to_all(pulled, "space", split_axis=0, concat_axis=0, tiled=True)
    placed = place_call(returned, cameras)
    grads = lax.all_to_all(placed, "view", split_axis=0, concat_axis=0, tiled=True)
    new_params, new_m, new_v = update_call(grads, params, adam_m, adam_v, visible.reshape(8, 128))
    return (image, new_params, new_m, new_v)


def solution(mesh):
    placed = (
        P(None, "space"),
        P(None, "space"),
        P(None, "space"),
        P("space"),
        P("view", None),
        P("view", "space", None),
        P("view", "space", None),
        P("view", "space", None),
        P("view", "space"),
        P("view", None, "space"),
    )
    return jax.shard_map(
        body,
        mesh=mesh,
        in_specs=placed,
        out_specs=(P("view", None, "space"), P(None, "space"), P(None, "space"), P(None, "space")),
        check_vma=False,
    )
```

```python
import functools

import jax
import jax.numpy as jnp
from jax import lax
from jax.experimental import pallas as pl
from jax.experimental.pallas import tpu as pltpu
from jax.sharding import PartitionSpec as P

focal_len = 1000.0
center_x = 512.0
harm_zero = 0.28209479177387814
harm_one = 0.4886025119029199
harm_two = (
    1.0925484305920792,
    -1.0925484305920792,
    0.31539156525252005,
    -1.0925484305920792,
    0.5462742152960396,
)
harm_three = (
    -0.5900435899266435,
    2.890611442640554,
    -0.4570457994644658,
    0.3731763325901154,
    -0.4570457994644658,
    1.445305721320277,
    -0.5900435899266435,
)
beta_one = 0.9
beta_two = 0.99
learn_rate = 0.05
adam_eps = 1e-08
adam_step = 100.0
num_param = 59
num_record = 11
num_view = 4
gauss_dev = 1024
shards = 128
cap = 4
slots = 512
slot_rows = 16
tile_dev = 2
list_len = 512


def project(gauss, camera, center_y):
    rotation = [[camera[3 * i + j] for j in range(3)] for i in range(3)]
    offset = [camera[9 + i] for i in range(3)]
    centre = [gauss[i] for i in range(3)]
    viewed = [sum((rotation[i][j] * centre[j] for j in range(3))) + offset[i] for i in range(3)]
    inverse = 1.0 / viewed[2]
    screen_x = focal_len * viewed[0] * inverse + center_x
    screen_y = focal_len * viewed[1] * inverse + center_y
    scales = [jnp.exp(gauss[3 + i]) for i in range(3)]
    length = jnp.sqrt(
        gauss[6] * gauss[6] + gauss[7] * gauss[7] + gauss[8] * gauss[8] + gauss[9] * gauss[9]
    )
    quat_w, quat_x, quat_y, quat_z = [gauss[6 + i] / length for i in range(4)]
    spin = [
        [
            1.0 - 2.0 * (quat_y * quat_y + quat_z * quat_z),
            2.0 * (quat_x * quat_y - quat_w * quat_z),
            2.0 * (quat_x * quat_z + quat_w * quat_y),
        ],
        [
            2.0 * (quat_x * quat_y + quat_w * quat_z),
            1.0 - 2.0 * (quat_x * quat_x + quat_z * quat_z),
            2.0 * (quat_y * quat_z - quat_w * quat_x),
        ],
        [
            2.0 * (quat_x * quat_z - quat_w * quat_y),
            2.0 * (quat_y * quat_z + quat_w * quat_x),
            1.0 - 2.0 * (quat_x * quat_x + quat_y * quat_y),
        ],
    ]
    factor = [[spin[i][j] * scales[j] for j in range(3)] for i in range(3)]
    sigma = [
        [sum((factor[i][j] * factor[k][j] for j in range(3))) for k in range(3)] for i in range(3)
    ]
    near = focal_len * inverse
    lean_x = -focal_len * viewed[0] * inverse * inverse
    lean_y = -focal_len * viewed[1] * inverse * inverse
    jacob = [
        [near * rotation[0][j] + lean_x * rotation[2][j] for j in range(3)],
        [near * rotation[1][j] + lean_y * rotation[2][j] for j in range(3)],
    ]
    halfway = [
        [sum((jacob[a][i] * sigma[i][k] for i in range(3))) for k in range(3)] for a in range(2)
    ]
    upper = sum((halfway[0][k] * jacob[0][k] for k in range(3))) + 0.3
    middle = sum((halfway[0][k] * jacob[1][k] for k in range(3)))
    lower = sum((halfway[1][k] * jacob[1][k] for k in range(3))) + 0.3
    determinant = upper * lower - middle * middle
    conic_a = lower / determinant
    conic_b = -middle / determinant
    conic_c = upper / determinant
    opacity = jax.nn.sigmoid(gauss[10])
    camera_pos = [-sum((rotation[i][j] * offset[i] for i in range(3))) for j in range(3)]
    toward = [centre[j] - camera_pos[j] for j in range(3)]
    reach = jnp.sqrt(toward[0] * toward[0] + toward[1] * toward[1] + toward[2] * toward[2])
    unit_x = toward[0] / reach
    unit_y = toward[1] / reach
    unit_z = toward[2] / reach
    square_x = unit_x * unit_x
    square_y = unit_y * unit_y
    square_z = unit_z * unit_z
    basis = [
        harm_zero + 0.0 * unit_x,
        -harm_one * unit_y,
        harm_one * unit_z,
        -harm_one * unit_x,
        harm_two[0] * unit_x * unit_y,
        harm_two[1] * unit_y * unit_z,
        harm_two[2] * (2.0 * square_z - square_x - square_y),
        harm_two[3] * unit_x * unit_z,
        harm_two[4] * (square_x - square_y),
        harm_three[0] * unit_y * (3.0 * square_x - square_y),
        harm_three[1] * unit_x * unit_y * unit_z,
        harm_three[2] * unit_y * (4.0 * square_z - square_x - square_y),
        harm_three[3] * unit_z * (2.0 * square_z - 3.0 * square_x - 3.0 * square_y),
        harm_three[4] * unit_x * (4.0 * square_z - square_x - square_y),
        harm_three[5] * unit_z * (square_x - square_y),
        harm_three[6] * unit_x * (square_x - 3.0 * square_y),
    ]
    colors = [0.5 + sum((basis[k] * gauss[11 + 16 * c + k] for k in range(16))) for c in range(3)]
    return [
        screen_x,
        screen_y,
        conic_a,
        conic_b,
        conic_c,
        opacity,
        colors[0],
        colors[1],
        colors[2],
        viewed[2],
        inverse,
    ]


def split_three(values):
    high = values.astype(jnp.bfloat16)
    left = values - high.astype(jnp.float32)
    middle = left.astype(jnp.bfloat16)
    low = (left - middle.astype(jnp.float32)).astype(jnp.bfloat16)
    return high, middle, low


def contract(left, right, left_dim, right_dim):
    return lax.dot_general(
        left,
        right,
        (((left_dim,), (right_dim,)), ((), ())),
        preferred_element_type=jnp.float32,
    )


def as_mask(condition):
    return jnp.where(condition, 1.0, 0.0).astype(jnp.bfloat16)


def send_kernel(center_y, params, route, count, camera, out, turned):
    rows = params[...].reshape(num_param, 8, 128)
    cam = [camera[0, i] for i in range(12)]
    records = project([rows[i] for i in range(num_param)], cam, center_y)
    table = jnp.concatenate(split_three(jnp.concatenate(records, axis=0)), axis=0)
    chosen = route[0]
    sub = lax.broadcasted_iota(jnp.int32, (128, slots), 0)
    picked = contract(table, as_mask(sub == (chosen & 127)), 1, 0)
    size = 8 * num_record
    picked = picked[0:size] + (picked[size : 2 * size] + picked[2 * size :])
    high = lax.broadcasted_iota(jnp.int32, (8, slots), 0) == (chosen >> 7)
    sent = [
        jnp.sum(jnp.where(high, picked[8 * r : 8 * r + 8], 0.0), axis=0, keepdims=True)
        for r in range(num_record)
    ]
    sent.append((chosen + 1).astype(jnp.float32))
    sent.append(jnp.zeros((slot_rows - num_record - 1, slots), jnp.float32))
    sent = jnp.concatenate(sent, axis=0)
    turned[:, 0:slot_rows] = sent.T
    parts = [turned[pl.ds(c, shards, stride=cap), :][:, 0:slot_rows] for c in range(cap)]
    width = cap * slot_rows
    spread = jnp.concatenate(parts + [jnp.zeros((shards, 128 - width), jnp.float32)], axis=1)
    used = jnp.broadcast_to(count[0], (8, shards)).T[:, 0:1]
    lane = lax.broadcasted_iota(jnp.int32, (shards, 128), 1)
    out[...] = jnp.where((lane >> 4) < used, spread, 0.0)


def tile_kernel(arrived, lists, places, target, camera, image, out):
    turned = arrived[...].T
    rec = jnp.concatenate([turned[c * slot_rows : (c + 1) * slot_rows] for c in range(cap)], axis=1)
    order = jnp.concatenate([lists[0, t : t + 1] for t in range(tile_dev)], axis=1)
    total = tile_dev * list_len
    source = lax.broadcasted_iota(jnp.int32, (shards, total), 0)
    found = as_mask(source == (order >> 2))
    number = lax.broadcasted_iota(jnp.int32, (8, total), 1) + 1
    row = lax.broadcasted_iota(jnp.int32, (8, total), 0)
    digits = jnp.where(row < 4, number >> 8, number & 255)
    digits = jnp.where((order & 3) == (row & 3), digits, 0).astype(jnp.float32)
    keys = contract(digits.astype(jnp.bfloat16), found, 1, 1)
    keys = 256.0 * keys[0:4] + keys[4:8]
    key = jnp.concatenate([keys[c : c + 1] for c in range(cap)], axis=1)
    key_col = jnp.broadcast_to(key, (8, slots)).T[:, 0:1]
    second = key > float(list_len)
    floor = jnp.where(second, float(list_len), 0.0)
    before = as_mask((key_col < key) & (key_col > floor))
    corner_x = [((places[0, t] & 63) * 16).astype(jnp.float32) + 8.0 for t in range(tile_dev)]
    corner_y = [((places[0, t] >> 6) * 16).astype(jnp.float32) + 8.0 for t in range(tile_dev)]
    at_x = rec[0:1] - jnp.where(second, corner_x[1], corner_x[0])
    at_y = rec[1:2] - jnp.where(second, corner_y[1], corner_y[0])
    con_a, con_b, con_c = rec[2:3], rec[3:4], rec[4:5]
    opacity = jnp.where(key > 0.0, rec[5:6], 0.0)
    lane = lax.broadcasted_iota(jnp.int32, (256, 1), 0)
    pix_x = (lane & 15).astype(jnp.float32) - 7.5
    pix_y = (lane >> 4).astype(jnp.float32) - 7.5
    apart_x = pix_x - at_x
    apart_y = pix_y - at_y
    half_a, half_c = -0.5 * con_a, -0.5 * con_c
    power = apart_x * (half_a * apart_x - con_b * apart_y) + half_c * apart_y * apart_y
    alpha = opacity * jnp.exp(power)
    keep = 1.0 - alpha
    logs = jnp.concatenate(split_three(jnp.log(keep)), axis=0)
    sums = contract(logs, before, 1, 0)
    through = jnp.exp(sums[0:256] + (sums[256:512] + sums[512:768]))
    weight = alpha * through
    w_hi, w_mid, w_lo = split_three(weight)
    feats = rec[6:11]
    gap = jnp.zeros((3, slots), jnp.float32)
    feats = jnp.concatenate(
        [jnp.where(second, 0.0, feats), gap, jnp.where(second, feats, 0.0), gap], axis=0
    )
    f_hi, f_mid, f_lo = split_three(feats)
    f_all = jnp.concatenate([f_hi, f_mid, f_lo], axis=0)
    drawn_hi = contract(f_all, w_hi, 1, 1)
    drawn_mid = contract(f_all[0:32], w_mid, 1, 1)
    drawn_lo = contract(f_all[0:16], w_lo, 1, 1)
    drawn = drawn_hi[0:16] + (
        (drawn_hi[16:32] + drawn_mid[0:16]) + (drawn_hi[32:48] + drawn_mid[16:32] + drawn_lo)
    )
    shown = jnp.concatenate([drawn[0:5], drawn[8:13]], axis=1)
    for ch in range(5):
        image[ch] = shown[ch : ch + 1]
    diff = shown - jnp.concatenate([target[ch] for ch in range(5)], axis=0)
    gap = jnp.zeros((3, 256), jnp.float32)
    residue = jnp.concatenate([diff[:, 0:256], gap, diff[:, 256:512], gap], axis=0)
    g_hi, g_mid, g_lo = split_three(residue)
    g_six = jnp.concatenate([g_hi, g_hi, g_mid, g_mid, g_hi, g_lo], axis=0)
    f_six = jnp.concatenate([f_hi, f_mid, f_hi, f_mid, f_lo, f_hi], axis=0)
    score = contract(g_six, f_six, 0, 0)
    tails = contract(jnp.concatenate(split_three(weight * score), axis=0), before, 1, 1)
    tail = tails[0:256] + (tails[256:512] + tails[512:768])
    pull = alpha * (through * score - tail / keep)
    seat = lax.broadcasted_iota(jnp.int32, (8, 256), 1)
    row = lax.broadcasted_iota(jnp.int32, (8, 256), 0)
    seat_x = (seat & 15).astype(jnp.float32) - 7.5
    seat_y = (seat >> 4).astype(jnp.float32) - 7.5
    first = jnp.where((row == 1) | (row == 3) | (row == 4), seat_x, 1.0)
    first = jnp.where((row == 2) | (row == 5), seat_y, first)
    other = jnp.where(row == 3, seat_x, 1.0)
    other = jnp.where((row == 4) | (row == 5), seat_y, other)
    basis = (first * other).astype(jnp.bfloat16)
    moments = contract(
        jnp.concatenate([basis] * 3, axis=1), jnp.concatenate(split_three(pull), axis=0), 1, 0
    )
    m_0, m_x, m_y, m_xx, m_xy, m_yy = [moments[i : i + 1] for i in range(6)]
    d_x = m_x - at_x * m_0
    d_y = m_y - at_y * m_0
    d_xx = m_xx - at_x * (m_x + d_x)
    d_xy = m_xy - at_x * m_y - at_y * d_x
    d_yy = m_yy - at_y * (m_y + d_y)
    g_all = jnp.concatenate([g_hi, g_mid, g_lo], axis=0)
    color_hi = contract(g_all, w_hi, 1, 0)
    color_mid = contract(g_all[0:32], w_mid, 1, 0)
    color_lo = contract(g_all[0:16], w_lo, 1, 0)
    color = color_hi[0:16] + (
        (color_hi[16:32] + color_mid[0:16]) + (color_hi[32:48] + color_mid[16:32] + color_lo)
    )
    color = jnp.where(second, color[8:13], color[0:5])
    pulled = jnp.concatenate(
        [
            con_a * d_x + con_b * d_y,
            con_b * d_x + con_c * d_y,
            -0.5 * d_xx,
            -d_xy,
            -0.5 * d_yy,
            jnp.where(opacity > 0.0, m_0 / jnp.where(opacity > 0.0, opacity, 1.0), 0.0),
            color,
            rec[11:12],
            jnp.zeros((4, slots), jnp.float32),
        ],
        axis=0,
    )
    stacked = [pulled[:, c * shards : (c + 1) * shards] for c in range(cap)]
    stacked += [jnp.full((1, shards), camera[0, i], jnp.float32) for i in range(12)]
    stacked.append(jnp.zeros((128 - cap * slot_rows - 12, shards), jnp.float32))
    block = jnp.concatenate(stacked, axis=0).T
    for w in range(num_view):
        out[w] = block


def update_kernel(center_y, grads, params, adam_m, adam_v, visible, new_p, new_m, new_v):
    turned = [grads[w].T for w in range(num_view)]
    slot = [turned[w][c * slot_rows : (c + 1) * slot_rows] for w in range(num_view) for c in range(cap)]
    slot = jnp.concatenate(slot, axis=1)
    total = num_view * slots
    number = slot[num_record : num_record + 1].astype(jnp.int32) - 1
    viewer = (lax.broadcasted_iota(jnp.int32, (1, total), 1) >> 9).astype(jnp.float32) + 1.0
    high = lax.broadcasted_iota(jnp.int32, (8, total), 0) == (number >> 7)
    place = as_mask(lax.broadcasted_iota(jnp.int32, (128, total), 0) == (number & 127))
    spread = [jnp.where(high, slot[r : r + 1], 0.0) for r in range(num_record)]
    spread.append(jnp.where(high, viewer, 0.0))
    spread = jnp.concatenate(split_three(jnp.concatenate(spread, axis=0)), axis=0)
    placed = contract(spread, place, 1, 1)
    size = 8 * (num_record + 1)
    placed = placed[0:size] + (placed[size : 2 * size] + placed[2 * size :])
    pulled = [placed[8 * r : 8 * r + 8] for r in range(num_record)]
    seen = placed[8 * num_record :]
    base = cap * slot_rows
    cam = []
    for i in range(12):
        value = jnp.broadcast_to(turned[0][base + i : base + i + 1], (8, 128))
        for w in range(1, num_view):
            value = jnp.where(seen == w + 1.0, turned[w][base + i : base + i + 1], value)
        cam.append(value)
    rows = params[...].reshape(num_param, 8, 128)
    _, pull = jax.vjp(
        lambda *gauss: project(gauss, cam, center_y), *[rows[i] for i in range(num_param)]
    )
    grad = jnp.stack(pull(pulled)).reshape(num_param, gauss_dev)
    keep = jnp.broadcast_to(visible[...].reshape(1, gauss_dev) > 0, grad.shape)
    old, old_m, old_v = params[...], adam_m[...], adam_v[...]
    moment_one = beta_one * old_m + (1.0 - beta_one) * grad
    moment_two = beta_two * old_v + (1.0 - beta_two) * grad * grad
    first_hat = moment_one / (1.0 - beta_one**adam_step)
    second_hat = moment_two / (1.0 - beta_two**adam_step)
    stepped = old - learn_rate * first_hat / (jnp.sqrt(second_hat) + adam_eps)
    new_p[...] = jnp.where(keep, stepped, old)
    new_m[...] = jnp.where(keep, moment_one, old_m)
    new_v[...] = jnp.where(keep, moment_two, old_v)


def shaped(*dims):
    return jax.ShapeDtypeStruct(dims, jnp.float32)


vector = pl.BlockSpec(memory_space=pltpu.VMEM)
scalar = pl.BlockSpec(memory_space=pltpu.SMEM)


def send_call(params, send_index, send_count, cameras):
    return pl.pallas_call(
        functools.partial(send_kernel, 8.0 * (tile_dev * shards) / 64.0),
        out_shape=shaped(shards, 128),
        in_specs=[vector, vector, vector, scalar],
        scratch_shapes=[pltpu.VMEM((slots, 128), jnp.float32)],
        name="send",
    )(params, send_index, send_count, cameras)


def tile_call(arrived, tile_lists, tile_pos, target, cameras):
    return pl.pallas_call(
        tile_kernel,
        out_shape=(shaped(5, 1, tile_dev * 256), shaped(num_view, shards, 128)),
        in_specs=[vector, vector, scalar, vector, scalar],
        name="tiles",
    )(arrived, tile_lists, tile_pos, target, cameras)


def update_call(grads, params, adam_m, adam_v, visible):
    return pl.pallas_call(
        functools.partial(update_kernel, 8.0 * (tile_dev * shards) / 64.0),
        out_shape=(shaped(num_param, gauss_dev),) * 3,
        in_specs=[vector] * 5,
        name="update",
    )(grads, params, adam_m, adam_v, visible)


def body(
    params, adam_m, adam_v, visible, cameras, send_index, send_count, tile_lists, tile_pos, target
):
    sending = send_call(params, send_index, send_count, cameras)
    arrived = lax.all_to_all(sending, "space", split_axis=0, concat_axis=0, tiled=True)
    wanted = jnp.transpose(target, (1, 0, 2))
    image, pulled = tile_call(arrived, tile_lists, tile_pos, wanted, cameras)
    image = jnp.transpose(image, (1, 0, 2))
    pulled = pulled.reshape(num_view * shards, 128)
    grads = lax.all_to_all(pulled, ("view", "space"), split_axis=0, concat_axis=0, tiled=True)
    grads = grads.reshape(num_view, shards, 128)
    new_params, new_m, new_v = update_call(grads, params, adam_m, adam_v, visible.reshape(8, 128))
    return (image, new_params, new_m, new_v)


def solution(mesh):
    placed = (
        P(None, "space"),
        P(None, "space"),
        P(None, "space"),
        P("space"),
        P("view", None),
        P("view", "space", None),
        P("view", "space", None),
        P("view", "space", None),
        P("view", "space"),
        P("view", None, "space"),
    )
    return jax.shard_map(
        body,
        mesh=mesh,
        in_specs=placed,
        out_specs=(P("view", None, "space"), P(None, "space"), P(None, "space"), P(None, "space")),
        check_vma=False,
    )
```

```python
import functools

import jax
import jax.numpy as jnp
from jax import lax
from jax.experimental import pallas as pl
from jax.experimental.pallas import tpu as pltpu
from jax.sharding import PartitionSpec as P

focal_len = 1000.0
center_x = 512.0
harm_zero = 0.28209479177387814
harm_one = 0.4886025119029199
harm_two = (
    1.0925484305920792,
    -1.0925484305920792,
    0.31539156525252005,
    -1.0925484305920792,
    0.5462742152960396,
)
harm_three = (
    -0.5900435899266435,
    2.890611442640554,
    -0.4570457994644658,
    0.3731763325901154,
    -0.4570457994644658,
    1.445305721320277,
    -0.5900435899266435,
)
beta_one = 0.9
beta_two = 0.99
learn_rate = 0.05
adam_eps = 1e-08
adam_step = 100.0
num_param = 59
num_record = 11
num_view = 4
gauss_dev = 1024
shards = 128
cap = 4
slots = 512
slot_rows = 16
tile_dev = 2
list_len = 512


def project(gauss, camera, center_y):
    rotation = [[camera[3 * i + j] for j in range(3)] for i in range(3)]
    offset = [camera[9 + i] for i in range(3)]
    centre = [gauss[i] for i in range(3)]
    viewed = [sum((rotation[i][j] * centre[j] for j in range(3))) + offset[i] for i in range(3)]
    inverse = 1.0 / viewed[2]
    screen_x = focal_len * viewed[0] * inverse + center_x
    screen_y = focal_len * viewed[1] * inverse + center_y
    scales = [jnp.exp(gauss[3 + i]) for i in range(3)]
    length = jnp.sqrt(
        gauss[6] * gauss[6] + gauss[7] * gauss[7] + gauss[8] * gauss[8] + gauss[9] * gauss[9]
    )
    quat_w, quat_x, quat_y, quat_z = [gauss[6 + i] / length for i in range(4)]
    spin = [
        [
            1.0 - 2.0 * (quat_y * quat_y + quat_z * quat_z),
            2.0 * (quat_x * quat_y - quat_w * quat_z),
            2.0 * (quat_x * quat_z + quat_w * quat_y),
        ],
        [
            2.0 * (quat_x * quat_y + quat_w * quat_z),
            1.0 - 2.0 * (quat_x * quat_x + quat_z * quat_z),
            2.0 * (quat_y * quat_z - quat_w * quat_x),
        ],
        [
            2.0 * (quat_x * quat_z - quat_w * quat_y),
            2.0 * (quat_y * quat_z + quat_w * quat_x),
            1.0 - 2.0 * (quat_x * quat_x + quat_y * quat_y),
        ],
    ]
    factor = [[spin[i][j] * scales[j] for j in range(3)] for i in range(3)]
    sigma = [
        [sum((factor[i][j] * factor[k][j] for j in range(3))) for k in range(3)] for i in range(3)
    ]
    near = focal_len * inverse
    lean_x = -focal_len * viewed[0] * inverse * inverse
    lean_y = -focal_len * viewed[1] * inverse * inverse
    jacob = [
        [near * rotation[0][j] + lean_x * rotation[2][j] for j in range(3)],
        [near * rotation[1][j] + lean_y * rotation[2][j] for j in range(3)],
    ]
    halfway = [
        [sum((jacob[a][i] * sigma[i][k] for i in range(3))) for k in range(3)] for a in range(2)
    ]
    upper = sum((halfway[0][k] * jacob[0][k] for k in range(3))) + 0.3
    middle = sum((halfway[0][k] * jacob[1][k] for k in range(3)))
    lower = sum((halfway[1][k] * jacob[1][k] for k in range(3))) + 0.3
    determinant = upper * lower - middle * middle
    conic_a = lower / determinant
    conic_b = -middle / determinant
    conic_c = upper / determinant
    opacity = jax.nn.sigmoid(gauss[10])
    camera_pos = [-sum((rotation[i][j] * offset[i] for i in range(3))) for j in range(3)]
    toward = [centre[j] - camera_pos[j] for j in range(3)]
    reach = jnp.sqrt(toward[0] * toward[0] + toward[1] * toward[1] + toward[2] * toward[2])
    unit_x = toward[0] / reach
    unit_y = toward[1] / reach
    unit_z = toward[2] / reach
    square_x = unit_x * unit_x
    square_y = unit_y * unit_y
    square_z = unit_z * unit_z
    basis = [
        harm_zero + 0.0 * unit_x,
        -harm_one * unit_y,
        harm_one * unit_z,
        -harm_one * unit_x,
        harm_two[0] * unit_x * unit_y,
        harm_two[1] * unit_y * unit_z,
        harm_two[2] * (2.0 * square_z - square_x - square_y),
        harm_two[3] * unit_x * unit_z,
        harm_two[4] * (square_x - square_y),
        harm_three[0] * unit_y * (3.0 * square_x - square_y),
        harm_three[1] * unit_x * unit_y * unit_z,
        harm_three[2] * unit_y * (4.0 * square_z - square_x - square_y),
        harm_three[3] * unit_z * (2.0 * square_z - 3.0 * square_x - 3.0 * square_y),
        harm_three[4] * unit_x * (4.0 * square_z - square_x - square_y),
        harm_three[5] * unit_z * (square_x - square_y),
        harm_three[6] * unit_x * (square_x - 3.0 * square_y),
    ]
    colors = [0.5 + sum((basis[k] * gauss[11 + 16 * c + k] for k in range(16))) for c in range(3)]
    return [
        screen_x,
        screen_y,
        conic_a,
        conic_b,
        conic_c,
        opacity,
        colors[0],
        colors[1],
        colors[2],
        viewed[2],
        inverse,
    ]


def split_three(values):
    high = values.astype(jnp.bfloat16)
    left = values - high.astype(jnp.float32)
    middle = left.astype(jnp.bfloat16)
    low = (left - middle.astype(jnp.float32)).astype(jnp.bfloat16)
    return high, middle, low


def contract(left, right, left_dim, right_dim):
    return lax.dot_general(
        left,
        right,
        (((left_dim,), (right_dim,)), ((), ())),
        preferred_element_type=jnp.float32,
    )


def as_mask(condition):
    return jnp.where(condition, 1.0, 0.0).astype(jnp.bfloat16)


def send_kernel(center_y, params, route, count, camera, out, turned):
    rows = params[...].reshape(num_param, 8, 128)
    cam = [camera[0, i] for i in range(12)]
    records = project([rows[i] for i in range(num_param)], cam, center_y)
    table = jnp.concatenate(split_three(jnp.concatenate(records, axis=0)), axis=0)
    chosen = route[0]
    sub = lax.broadcasted_iota(jnp.int32, (128, slots), 0)
    picked = contract(table, as_mask(sub == (chosen & 127)), 1, 0)
    size = 8 * num_record
    picked = picked[0:size] + (picked[size : 2 * size] + picked[2 * size :])
    high = lax.broadcasted_iota(jnp.int32, (8, slots), 0) == (chosen >> 7)
    sent = [
        jnp.sum(jnp.where(high, picked[8 * r : 8 * r + 8], 0.0), axis=0, keepdims=True)
        for r in range(num_record)
    ]
    sent.append((chosen + 1).astype(jnp.float32))
    sent.append(jnp.zeros((slot_rows - num_record - 1, slots), jnp.float32))
    sent = jnp.concatenate(sent, axis=0)
    turned[:, 0:slot_rows] = sent.T
    parts = [turned[pl.ds(c, shards, stride=cap), :][:, 0:slot_rows] for c in range(cap)]
    width = cap * slot_rows
    spread = jnp.concatenate(parts + [jnp.zeros((shards, 128 - width), jnp.float32)], axis=1)
    used = jnp.broadcast_to(count[0], (8, shards)).T[:, 0:1]
    lane = lax.broadcasted_iota(jnp.int32, (shards, 128), 1)
    out[...] = jnp.where((lane >> 4) < used, spread, 0.0)


def tile_kernel(arrived, lists, places, target, camera, image, out):
    turned = arrived[...].T
    rec = jnp.concatenate([turned[c * slot_rows : (c + 1) * slot_rows] for c in range(cap)], axis=1)
    order = jnp.concatenate([lists[0, t : t + 1] for t in range(tile_dev)], axis=1)
    total = tile_dev * list_len
    source = lax.broadcasted_iota(jnp.int32, (shards, total), 0)
    found = as_mask(source == (order >> 2))
    number = lax.broadcasted_iota(jnp.int32, (8, total), 1) + 1
    row = lax.broadcasted_iota(jnp.int32, (8, total), 0)
    digits = jnp.where(row < 4, number >> 8, number & 255)
    digits = jnp.where((order & 3) == (row & 3), digits, 0).astype(jnp.float32)
    keys = contract(digits.astype(jnp.bfloat16), found, 1, 1)
    keys = 256.0 * keys[0:4] + keys[4:8]
    key = jnp.concatenate([keys[c : c + 1] for c in range(cap)], axis=1)
    key_col = jnp.broadcast_to(key, (8, slots)).T[:, 0:1]
    second = key > float(list_len)
    floor = jnp.where(second, float(list_len), 0.0)
    before = as_mask((key_col < key) & (key_col > floor))
    corner_x = [((places[0, t] & 63) * 16).astype(jnp.float32) + 8.0 for t in range(tile_dev)]
    corner_y = [((places[0, t] >> 6) * 16).astype(jnp.float32) + 8.0 for t in range(tile_dev)]
    at_x = rec[0:1] - jnp.where(second, corner_x[1], corner_x[0])
    at_y = rec[1:2] - jnp.where(second, corner_y[1], corner_y[0])
    con_a, con_b, con_c = rec[2:3], rec[3:4], rec[4:5]
    opacity = jnp.where(key > 0.0, rec[5:6], 0.0)
    lane = lax.broadcasted_iota(jnp.int32, (256, 1), 0)
    pix_x = (lane & 15).astype(jnp.float32) - 7.5
    pix_y = (lane >> 4).astype(jnp.float32) - 7.5
    apart_x = pix_x - at_x
    apart_y = pix_y - at_y
    half_a, half_c = -0.5 * con_a, -0.5 * con_c
    power = apart_x * (half_a * apart_x - con_b * apart_y) + half_c * apart_y * apart_y
    alpha = opacity * jnp.exp(power)
    keep = 1.0 - alpha
    logs = jnp.concatenate(split_three(jnp.log(keep)), axis=0)
    sums = contract(logs, before, 1, 0)
    through = jnp.exp(sums[0:256] + (sums[256:512] + sums[512:768]))
    weight = alpha * through
    w_hi, w_mid, w_lo = split_three(weight)
    feats = rec[6:11]
    gap = jnp.zeros((3, slots), jnp.float32)
    feats = jnp.concatenate(
        [jnp.where(second, 0.0, feats), gap, jnp.where(second, feats, 0.0), gap], axis=0
    )
    f_hi, f_mid, f_lo = split_three(feats)
    f_all = jnp.concatenate([f_hi, f_mid, f_lo], axis=0)
    drawn_hi = contract(f_all, w_hi, 1, 1)
    drawn_mid = contract(f_all[0:32], w_mid, 1, 1)
    drawn_lo = contract(f_all[0:16], w_lo, 1, 1)
    drawn = drawn_hi[0:16] + (
        (drawn_hi[16:32] + drawn_mid[0:16]) + (drawn_hi[32:48] + drawn_mid[16:32] + drawn_lo)
    )
    shown = jnp.concatenate([drawn[0:5], drawn[8:13]], axis=1)
    for ch in range(5):
        image[ch] = shown[ch : ch + 1]
    diff = shown - jnp.concatenate([target[ch] for ch in range(5)], axis=0)
    gap = jnp.zeros((3, 256), jnp.float32)
    residue = jnp.concatenate([diff[:, 0:256], gap, diff[:, 256:512], gap], axis=0)
    g_hi, g_mid, g_lo = split_three(residue)
    g_six = jnp.concatenate([g_hi, g_hi, g_mid, g_mid, g_hi, g_lo], axis=0)
    f_six = jnp.concatenate([f_hi, f_mid, f_hi, f_mid, f_lo, f_hi], axis=0)
    score = contract(g_six, f_six, 0, 0)
    tails = contract(jnp.concatenate(split_three(weight * score), axis=0), before, 1, 1)
    tail = tails[0:256] + (tails[256:512] + tails[512:768])
    pull = alpha * (through * score - tail / keep)
    seat = lax.broadcasted_iota(jnp.int32, (8, 256), 1)
    row = lax.broadcasted_iota(jnp.int32, (8, 256), 0)
    seat_x = (seat & 15).astype(jnp.float32) - 7.5
    seat_y = (seat >> 4).astype(jnp.float32) - 7.5
    first = jnp.where((row == 1) | (row == 3) | (row == 4), seat_x, 1.0)
    first = jnp.where((row == 2) | (row == 5), seat_y, first)
    other = jnp.where(row == 3, seat_x, 1.0)
    other = jnp.where((row == 4) | (row == 5), seat_y, other)
    basis = (first * other).astype(jnp.bfloat16)
    moments = contract(
        jnp.concatenate([basis] * 3, axis=1), jnp.concatenate(split_three(pull), axis=0), 1, 0
    )
    m_0, m_x, m_y, m_xx, m_xy, m_yy = [moments[i : i + 1] for i in range(6)]
    d_x = m_x - at_x * m_0
    d_y = m_y - at_y * m_0
    d_xx = m_xx - at_x * (m_x + d_x)
    d_xy = m_xy - at_x * m_y - at_y * d_x
    d_yy = m_yy - at_y * (m_y + d_y)
    g_all = jnp.concatenate([g_hi, g_mid, g_lo], axis=0)
    color_hi = contract(g_all, w_hi, 1, 0)
    color_mid = contract(g_all[0:32], w_mid, 1, 0)
    color_lo = contract(g_all[0:16], w_lo, 1, 0)
    color = color_hi[0:16] + (
        (color_hi[16:32] + color_mid[0:16]) + (color_hi[32:48] + color_mid[16:32] + color_lo)
    )
    color = jnp.where(second, color[8:13], color[0:5])
    pulled = jnp.concatenate(
        [
            con_a * d_x + con_b * d_y,
            con_b * d_x + con_c * d_y,
            -0.5 * d_xx,
            -d_xy,
            -0.5 * d_yy,
            jnp.where(opacity > 0.0, m_0 / jnp.where(opacity > 0.0, opacity, 1.0), 0.0),
            color,
            rec[11:12],
            jnp.zeros((4, slots), jnp.float32),
        ],
        axis=0,
    )
    stacked = [pulled[:, c * shards : (c + 1) * shards] for c in range(cap)]
    stacked += [jnp.full((1, shards), camera[0, i], jnp.float32) for i in range(12)]
    stacked.append(jnp.zeros((128 - cap * slot_rows - 12, shards), jnp.float32))
    block = jnp.concatenate(stacked, axis=0).T
    for w in range(num_view):
        out[w] = block


def update_kernel(center_y, grads, params, adam_m, adam_v, visible, new_p, new_m, new_v):
    turned = [grads[w].T for w in range(num_view)]
    slot = [turned[w][c * slot_rows : (c + 1) * slot_rows] for w in range(num_view) for c in range(cap)]
    slot = jnp.concatenate(slot, axis=1)
    total = num_view * slots
    number = slot[num_record : num_record + 1].astype(jnp.int32) - 1
    viewer = (lax.broadcasted_iota(jnp.int32, (1, total), 1) >> 9).astype(jnp.float32) + 1.0
    high = lax.broadcasted_iota(jnp.int32, (8, total), 0) == (number >> 7)
    place = as_mask(lax.broadcasted_iota(jnp.int32, (128, total), 0) == (number & 127))
    spread = [jnp.where(high, slot[r : r + 1], 0.0) for r in range(num_record)]
    spread.append(jnp.where(high, viewer, 0.0))
    spread = jnp.concatenate(split_three(jnp.concatenate(spread, axis=0)), axis=0)
    placed = contract(spread, place, 1, 1)
    size = 8 * (num_record + 1)
    placed = placed[0:size] + (placed[size : 2 * size] + placed[2 * size :])
    pulled = [placed[8 * r : 8 * r + 8] for r in range(num_record)]
    seen = placed[8 * num_record :]
    base = cap * slot_rows
    cam = []
    for i in range(12):
        value = jnp.broadcast_to(turned[0][base + i : base + i + 1], (8, 128))
        for w in range(1, num_view):
            value = jnp.where(seen == w + 1.0, turned[w][base + i : base + i + 1], value)
        cam.append(value)
    rows = params[...].reshape(num_param, 8, 128)
    _, pull = jax.vjp(
        lambda *gauss: project(gauss, cam, center_y), *[rows[i] for i in range(num_param)]
    )
    grad = jnp.stack(pull(pulled)).reshape(num_param, gauss_dev)
    keep = jnp.broadcast_to(visible[...].reshape(1, gauss_dev) > 0, grad.shape)
    old, old_m, old_v = params[...], adam_m[...], adam_v[...]
    moment_one = beta_one * old_m + (1.0 - beta_one) * grad
    moment_two = beta_two * old_v + (1.0 - beta_two) * grad * grad
    first_hat = moment_one / (1.0 - beta_one**adam_step)
    second_hat = moment_two / (1.0 - beta_two**adam_step)
    stepped = old - learn_rate * first_hat / (jnp.sqrt(second_hat) + adam_eps)
    new_p[...] = jnp.where(keep, stepped, old)
    new_m[...] = jnp.where(keep, moment_one, old_m)
    new_v[...] = jnp.where(keep, moment_two, old_v)


def shaped(*dims):
    return jax.ShapeDtypeStruct(dims, jnp.float32)


def near(array):
    return pltpu.with_memory_space_constraint(array, pltpu.VMEM)


vector = pl.BlockSpec(memory_space=pltpu.VMEM)
scalar = pl.BlockSpec(memory_space=pltpu.SMEM)


def send_call(params, send_index, send_count, cameras):
    return pl.pallas_call(
        functools.partial(send_kernel, 8.0 * (tile_dev * shards) / 64.0),
        out_shape=pltpu.VMEM((shards, 128), jnp.float32),
        in_specs=[vector, vector, vector, scalar],
        scratch_shapes=[pltpu.VMEM((slots, 128), jnp.float32)],
        name="send",
    )(params, send_index, send_count, cameras)


def tile_call(arrived, tile_lists, tile_pos, target, cameras):
    return pl.pallas_call(
        tile_kernel,
        out_shape=(
            shaped(5, 1, tile_dev * 256),
            pltpu.VMEM((num_view, shards, 128), jnp.float32),
        ),
        in_specs=[vector, vector, scalar, vector, scalar],
        name="tiles",
    )(near(arrived), near(tile_lists), tile_pos, near(target), cameras)


def update_call(grads, params, adam_m, adam_v, visible):
    return pl.pallas_call(
        functools.partial(update_kernel, 8.0 * (tile_dev * shards) / 64.0),
        out_shape=(shaped(num_param, gauss_dev),) * 3,
        in_specs=[vector] * 5,
        name="update",
    )(near(grads), near(params), near(adam_m), near(adam_v), near(visible))


def body(
    params, adam_m, adam_v, visible, cameras, send_index, send_count, tile_lists, tile_pos, target
):
    sending = send_call(params, send_index, send_count, cameras)
    arrived = lax.all_to_all(sending, "space", split_axis=0, concat_axis=0, tiled=True)
    wanted = jnp.transpose(target, (1, 0, 2))
    image, pulled = tile_call(arrived, tile_lists, tile_pos, wanted, cameras)
    image = jnp.transpose(image, (1, 0, 2))
    pulled = pulled.reshape(num_view * shards, 128)
    grads = lax.all_to_all(pulled, ("view", "space"), split_axis=0, concat_axis=0, tiled=True)
    grads = grads.reshape(num_view, shards, 128)
    new_params, new_m, new_v = update_call(grads, params, adam_m, adam_v, visible.reshape(8, 128))
    return (image, new_params, new_m, new_v)


def solution(mesh):
    placed = (
        P(None, "space"),
        P(None, "space"),
        P(None, "space"),
        P("space"),
        P("view", None),
        P("view", "space", None),
        P("view", "space", None),
        P("view", "space", None),
        P("view", "space"),
        P("view", None, "space"),
    )
    return jax.shard_map(
        body,
        mesh=mesh,
        in_specs=placed,
        out_specs=(P("view", None, "space"), P(None, "space"), P(None, "space"), P(None, "space")),
        check_vma=False,
    )
```

```python
import functools

import jax
import jax.numpy as jnp
from jax import lax
from jax.experimental import pallas as pl
from jax.experimental.pallas import tpu as pltpu
from jax.sharding import PartitionSpec as P

focal_len = 1000.0
center_x = 512.0
harm_zero = 0.28209479177387814
harm_one = 0.4886025119029199
harm_two = (
    1.0925484305920792,
    -1.0925484305920792,
    0.31539156525252005,
    -1.0925484305920792,
    0.5462742152960396,
)
harm_three = (
    -0.5900435899266435,
    2.890611442640554,
    -0.4570457994644658,
    0.3731763325901154,
    -0.4570457994644658,
    1.445305721320277,
    -0.5900435899266435,
)
beta_one = 0.9
beta_two = 0.99
learn_rate = 0.05
adam_eps = 1e-08
adam_step = 100.0
num_param = 59
num_record = 11
num_view = 4
gauss_dev = 1024
shards = 128
cap = 4
slots = 512
slot_rows = 16
tile_dev = 2
list_len = 512
halves = 2


def project(gauss, camera, center_y):
    rotation = [[camera[3 * i + j] for j in range(3)] for i in range(3)]
    offset = [camera[9 + i] for i in range(3)]
    centre = [gauss[i] for i in range(3)]
    viewed = [sum((rotation[i][j] * centre[j] for j in range(3))) + offset[i] for i in range(3)]
    inverse = 1.0 / viewed[2]
    screen_x = focal_len * viewed[0] * inverse + center_x
    screen_y = focal_len * viewed[1] * inverse + center_y
    scales = [jnp.exp(gauss[3 + i]) for i in range(3)]
    length = jnp.sqrt(
        gauss[6] * gauss[6] + gauss[7] * gauss[7] + gauss[8] * gauss[8] + gauss[9] * gauss[9]
    )
    quat_w, quat_x, quat_y, quat_z = [gauss[6 + i] / length for i in range(4)]
    spin = [
        [
            1.0 - 2.0 * (quat_y * quat_y + quat_z * quat_z),
            2.0 * (quat_x * quat_y - quat_w * quat_z),
            2.0 * (quat_x * quat_z + quat_w * quat_y),
        ],
        [
            2.0 * (quat_x * quat_y + quat_w * quat_z),
            1.0 - 2.0 * (quat_x * quat_x + quat_z * quat_z),
            2.0 * (quat_y * quat_z - quat_w * quat_x),
        ],
        [
            2.0 * (quat_x * quat_z - quat_w * quat_y),
            2.0 * (quat_y * quat_z + quat_w * quat_x),
            1.0 - 2.0 * (quat_x * quat_x + quat_y * quat_y),
        ],
    ]
    factor = [[spin[i][j] * scales[j] for j in range(3)] for i in range(3)]
    sigma = [
        [sum((factor[i][j] * factor[k][j] for j in range(3))) for k in range(3)] for i in range(3)
    ]
    near = focal_len * inverse
    lean_x = -focal_len * viewed[0] * inverse * inverse
    lean_y = -focal_len * viewed[1] * inverse * inverse
    jacob = [
        [near * rotation[0][j] + lean_x * rotation[2][j] for j in range(3)],
        [near * rotation[1][j] + lean_y * rotation[2][j] for j in range(3)],
    ]
    halfway = [
        [sum((jacob[a][i] * sigma[i][k] for i in range(3))) for k in range(3)] for a in range(2)
    ]
    upper = sum((halfway[0][k] * jacob[0][k] for k in range(3))) + 0.3
    middle = sum((halfway[0][k] * jacob[1][k] for k in range(3)))
    lower = sum((halfway[1][k] * jacob[1][k] for k in range(3))) + 0.3
    determinant = upper * lower - middle * middle
    conic_a = lower / determinant
    conic_b = -middle / determinant
    conic_c = upper / determinant
    opacity = jax.nn.sigmoid(gauss[10])
    camera_pos = [-sum((rotation[i][j] * offset[i] for i in range(3))) for j in range(3)]
    toward = [centre[j] - camera_pos[j] for j in range(3)]
    reach = jnp.sqrt(toward[0] * toward[0] + toward[1] * toward[1] + toward[2] * toward[2])
    unit_x = toward[0] / reach
    unit_y = toward[1] / reach
    unit_z = toward[2] / reach
    square_x = unit_x * unit_x
    square_y = unit_y * unit_y
    square_z = unit_z * unit_z
    basis = [
        harm_zero + 0.0 * unit_x,
        -harm_one * unit_y,
        harm_one * unit_z,
        -harm_one * unit_x,
        harm_two[0] * unit_x * unit_y,
        harm_two[1] * unit_y * unit_z,
        harm_two[2] * (2.0 * square_z - square_x - square_y),
        harm_two[3] * unit_x * unit_z,
        harm_two[4] * (square_x - square_y),
        harm_three[0] * unit_y * (3.0 * square_x - square_y),
        harm_three[1] * unit_x * unit_y * unit_z,
        harm_three[2] * unit_y * (4.0 * square_z - square_x - square_y),
        harm_three[3] * unit_z * (2.0 * square_z - 3.0 * square_x - 3.0 * square_y),
        harm_three[4] * unit_x * (4.0 * square_z - square_x - square_y),
        harm_three[5] * unit_z * (square_x - square_y),
        harm_three[6] * unit_x * (square_x - 3.0 * square_y),
    ]
    colors = [0.5 + sum((basis[k] * gauss[11 + 16 * c + k] for k in range(16))) for c in range(3)]
    return [
        screen_x,
        screen_y,
        conic_a,
        conic_b,
        conic_c,
        opacity,
        colors[0],
        colors[1],
        colors[2],
        viewed[2],
        inverse,
    ]


def split_three(values):
    high = values.astype(jnp.bfloat16)
    left = values - high.astype(jnp.float32)
    middle = left.astype(jnp.bfloat16)
    low = (left - middle.astype(jnp.float32)).astype(jnp.bfloat16)
    return high, middle, low


def split_two(values):
    high = values.astype(jnp.bfloat16)
    return high, (values - high.astype(jnp.float32)).astype(jnp.bfloat16)


def contract(left, right, left_dim, right_dim):
    return lax.dot_general(
        left,
        right,
        (((left_dim,), (right_dim,)), ((), ())),
        preferred_element_type=jnp.float32,
    )


def as_mask(condition):
    return jnp.where(condition, 1.0, 0.0).astype(jnp.bfloat16)


def send_kernel(center_y, params, route, count, camera, out, turned):
    rows = params[...].reshape(num_param, 8, 128)
    cam = [camera[0, i] for i in range(12)]
    records = project([rows[i] for i in range(num_param)], cam, center_y)
    table = jnp.concatenate(split_three(jnp.concatenate(records, axis=0)), axis=0)
    chosen = route[0]
    sub = lax.broadcasted_iota(jnp.int32, (128, slots), 0)
    picked = contract(table, as_mask(sub == (chosen & 127)), 1, 0)
    size = 8 * num_record
    picked = picked[0:size] + (picked[size : 2 * size] + picked[2 * size :])
    high = lax.broadcasted_iota(jnp.int32, (8, slots), 0) == (chosen >> 7)
    sent = [
        jnp.sum(jnp.where(high, picked[8 * r : 8 * r + 8], 0.0), axis=0, keepdims=True)
        for r in range(num_record)
    ]
    sent.append((chosen + 1).astype(jnp.float32))
    sent.append(jnp.zeros((slot_rows - num_record - 1, slots), jnp.float32))
    sent = jnp.concatenate(sent, axis=0)
    turned[:, 0:slot_rows] = sent.T
    parts = [turned[pl.ds(c, shards, stride=cap), :][:, 0:slot_rows] for c in range(cap)]
    width = cap * slot_rows
    spread = jnp.concatenate(parts + [jnp.zeros((shards, 128 - width), jnp.float32)], axis=1)
    used = jnp.broadcast_to(count[0], (8, shards)).T[:, 0:1]
    lane = lax.broadcasted_iota(jnp.int32, (shards, 128), 1)
    out[...] = jnp.where((lane >> 4) < used, spread, 0.0)


def order_kernel(lists, key_out, before_out):
    order = jnp.concatenate([lists[0, t : t + 1] for t in range(tile_dev)], axis=1)
    total = tile_dev * list_len
    source = lax.broadcasted_iota(jnp.int32, (shards, total), 0)
    found = as_mask(source == (order >> 2))
    number = lax.broadcasted_iota(jnp.int32, (8, total), 1) + 1
    row = lax.broadcasted_iota(jnp.int32, (8, total), 0)
    digits = jnp.where(row < 4, number >> 8, number & 255)
    digits = jnp.where((order & 3) == (row & 3), digits, 0).astype(jnp.float32)
    keys = contract(digits.astype(jnp.bfloat16), found, 1, 1)
    keys = 256.0 * keys[0:4] + keys[4:8]
    key = jnp.concatenate([keys[c : c + 1] for c in range(cap)], axis=1)
    key_all = jnp.broadcast_to(key, (8, slots))
    key_col = key_all.T[:, 0:1]
    floor = jnp.where(key > float(list_len), float(list_len), 0.0)
    key_out[...] = key_all
    before_out[...] = as_mask((key_col < key) & (key_col > floor))


def tile_kernel(arrived, keys, before_in, places, target, camera, image, out):
    turned = arrived[...].T
    rec = jnp.concatenate([turned[c * slot_rows : (c + 1) * slot_rows] for c in range(cap)], axis=1)
    key = keys[0:1]
    second = key > float(list_len)
    before = before_in[...]
    corner_x = [((places[0, t] & 63) * 16).astype(jnp.float32) + 8.0 for t in range(tile_dev)]
    corner_y = [((places[0, t] >> 6) * 16).astype(jnp.float32) + 8.0 for t in range(tile_dev)]
    at_x = rec[0:1] - jnp.where(second, corner_x[1], corner_x[0])
    at_y = rec[1:2] - jnp.where(second, corner_y[1], corner_y[0])
    con_a, con_b, con_c = rec[2:3], rec[3:4], rec[4:5]
    half_a, half_c = -0.5 * con_a, -0.5 * con_c
    opacity = jnp.where(key > 0.0, rec[5:6], 0.0)
    feats = rec[6:11]
    gap = jnp.zeros((3, slots), jnp.float32)
    feats = jnp.concatenate(
        [jnp.where(second, 0.0, feats), gap, jnp.where(second, feats, 0.0), gap], axis=0
    )
    f_hi, f_lo, f_last = split_three(feats)
    f_both = jnp.concatenate([f_hi, f_lo], axis=0)
    f_six = jnp.concatenate([f_hi, f_lo, f_hi, f_lo, f_last, f_hi], axis=0)
    size = 256 // halves
    rows = range(halves)
    lane = lax.broadcasted_iota(jnp.int32, (size, 1), 0)
    pix_x = (lane & 15).astype(jnp.float32) - 7.5
    pix_y = (lane >> 4).astype(jnp.float32)
    seat = lax.broadcasted_iota(jnp.int32, (8, size), 1)
    row = lax.broadcasted_iota(jnp.int32, (8, size), 0)
    seat_x = (seat & 15).astype(jnp.float32) - 7.5
    gap = jnp.zeros((3, size), jnp.float32)

    def shade(i):
        apart_x = pix_x - at_x
        apart_y = (pix_y + (i * size // 16 - 7.5)) - at_y
        power = apart_x * (half_a * apart_x - con_b * apart_y) + half_c * apart_y * apart_y
        alpha = opacity * jnp.exp(power)
        keep = 1.0 - alpha
        return alpha, keep, jnp.concatenate(split_two(jnp.log(keep)), axis=0)

    def blend(i, alpha, logs):
        sums = contract(logs, before, 1, 0)
        through = jnp.exp(sums[0:size] + sums[size:])
        weight = alpha * through
        return through, weight, split_two(weight)

    def draw(i, w_hi, w_lo):
        drawn = contract(f_both, w_hi, 1, 1)
        drawn = drawn[0:16] + (drawn[16:32] + contract(f_hi, w_lo, 1, 1))
        parts = []
        for t in range(tile_dev):
            shown = drawn[8 * t : 8 * t + 5]
            spot = pl.ds(t * 256 + i * size, size)
            for ch in range(5):
                image[ch, :, spot] = shown[ch : ch + 1]
            wanted = jnp.concatenate([target[ch, :, spot] for ch in range(5)], axis=0)
            parts += [shown - wanted, gap]
        return split_three(jnp.concatenate(parts, axis=0))

    def score_of(g_hi, g_lo, g_last, weight):
        score = contract(
            jnp.concatenate([g_hi, g_hi, g_lo, g_lo, g_hi, g_last], axis=0), f_six, 0, 0
        )
        return score, jnp.concatenate(split_two(weight * score), axis=0)

    def pull_of(alpha, keep, through, score, tails):
        tail = contract(tails, before, 1, 1)
        tail = tail[0:size] + tail[size:]
        return jnp.concatenate(split_three(alpha * (through * score - tail / keep)), axis=0)

    def moments_of(i, pull):
        seat_y = (seat >> 4).astype(jnp.float32) + (i * size // 16 - 7.5)
        first = jnp.where((row == 1) | (row == 3) | (row == 4), seat_x, 1.0)
        first = jnp.where((row == 2) | (row == 5), seat_y, first)
        other = jnp.where(row == 3, seat_x, 1.0)
        other = jnp.where((row == 4) | (row == 5), seat_y, other)
        basis = (first * other).astype(jnp.bfloat16)
        return contract(jnp.concatenate([basis] * 3, axis=1), pull, 1, 0)

    def colors_of(g_hi, g_lo, g_last, w_hi, w_lo):
        color = contract(jnp.concatenate([g_hi, g_lo], axis=0), w_hi, 1, 0)
        return color[0:16] + (color[16:32] + contract(g_hi, w_lo, 1, 0))

    shaded = [shade(i) for i in rows]
    blended = [blend(i, shaded[i][0], shaded[i][2]) for i in rows]
    diffs = [draw(i, *blended[i][2]) for i in rows]
    scores = [score_of(*diffs[i], blended[i][1]) for i in rows]
    color = sum(colors_of(*diffs[i], *blended[i][2]) for i in rows)
    pulls = [
        pull_of(shaded[i][0], shaded[i][1], blended[i][0], scores[i][0], scores[i][1]) for i in rows
    ]
    moments = sum(moments_of(i, pulls[i]) for i in rows)
    m_0, m_x, m_y, m_xx, m_xy, m_yy = [moments[i : i + 1] for i in range(6)]
    d_x = m_x - at_x * m_0
    d_y = m_y - at_y * m_0
    d_xx = m_xx - at_x * (m_x + d_x)
    d_xy = m_xy - at_x * m_y - at_y * d_x
    d_yy = m_yy - at_y * (m_y + d_y)
    color = jnp.where(second, color[8:13], color[0:5])
    pulled = jnp.concatenate(
        [
            con_a * d_x + con_b * d_y,
            con_b * d_x + con_c * d_y,
            -0.5 * d_xx,
            -d_xy,
            -0.5 * d_yy,
            jnp.where(opacity > 0.0, m_0 / jnp.where(opacity > 0.0, opacity, 1.0), 0.0),
            color,
            rec[11:12],
            jnp.zeros((4, slots), jnp.float32),
        ],
        axis=0,
    )
    stacked = [pulled[:, c * shards : (c + 1) * shards] for c in range(cap)]
    stacked += [jnp.full((1, shards), camera[0, i], jnp.float32) for i in range(12)]
    stacked.append(jnp.zeros((128 - cap * slot_rows - 12, shards), jnp.float32))
    block = jnp.concatenate(stacked, axis=0).T
    for w in range(num_view):
        out[w] = block


def update_kernel(center_y, grads, params, adam_m, adam_v, visible, new_p, new_m, new_v):
    turned = [grads[w].T for w in range(num_view)]
    slot = [turned[w][c * slot_rows : (c + 1) * slot_rows] for w in range(num_view) for c in range(cap)]
    slot = jnp.concatenate(slot, axis=1)
    total = num_view * slots
    number = slot[num_record : num_record + 1].astype(jnp.int32) - 1
    viewer = (lax.broadcasted_iota(jnp.int32, (1, total), 1) >> 9).astype(jnp.float32) + 1.0
    high = lax.broadcasted_iota(jnp.int32, (8, total), 0) == (number >> 7)
    place = as_mask(lax.broadcasted_iota(jnp.int32, (128, total), 0) == (number & 127))
    coarse = slot.astype(jnp.bfloat16).astype(jnp.float32)
    fine = slot - coarse
    spread = [jnp.where(high, coarse[r : r + 1], 0.0) for r in range(num_record)]
    spread.append(jnp.where(high, viewer, 0.0))
    spread += [jnp.where(high, fine[r : r + 1], 0.0) for r in range(num_record)]
    placed = contract(jnp.concatenate(spread, axis=0).astype(jnp.bfloat16), place, 1, 1)
    size = 8 * num_record
    seen = placed[size : size + 8]
    placed = placed[0:size] + placed[size + 8 :]
    pulled = [placed[8 * r : 8 * r + 8] for r in range(num_record)]
    base = cap * slot_rows
    cam = []
    for i in range(12):
        value = jnp.broadcast_to(turned[0][base + i : base + i + 1], (8, 128))
        for w in range(1, num_view):
            value = jnp.where(seen == w + 1.0, turned[w][base + i : base + i + 1], value)
        cam.append(value)
    rows = params[...].reshape(num_param, 8, 128)
    _, pull = jax.vjp(
        lambda *gauss: project(gauss, cam, center_y), *[rows[i] for i in range(num_param)]
    )
    grad = jnp.stack(pull(pulled)).reshape(num_param, gauss_dev)
    keep = jnp.broadcast_to(visible[...].reshape(1, gauss_dev) > 0, grad.shape)
    old, old_m, old_v = params[...], adam_m[...], adam_v[...]
    moment_one = beta_one * old_m + (1.0 - beta_one) * grad
    moment_two = beta_two * old_v + (1.0 - beta_two) * grad * grad
    first_hat = moment_one / (1.0 - beta_one**adam_step)
    second_hat = moment_two / (1.0 - beta_two**adam_step)
    stepped = old - learn_rate * first_hat / (jnp.sqrt(second_hat) + adam_eps)
    new_p[...] = jnp.where(keep, stepped, old)
    new_m[...] = jnp.where(keep, moment_one, old_m)
    new_v[...] = jnp.where(keep, moment_two, old_v)


def shaped(*dims):
    return jax.ShapeDtypeStruct(dims, jnp.float32)


def near(array):
    return pltpu.with_memory_space_constraint(array, pltpu.VMEM)


vector = pl.BlockSpec(memory_space=pltpu.VMEM)
scalar = pl.BlockSpec(memory_space=pltpu.SMEM)


def send_call(params, send_index, send_count, cameras):
    return pl.pallas_call(
        functools.partial(send_kernel, 8.0 * (tile_dev * shards) / 64.0),
        out_shape=pltpu.VMEM((shards, 128), jnp.float32),
        in_specs=[vector, vector, vector, scalar],
        scratch_shapes=[pltpu.VMEM((slots, 128), jnp.float32)],
        name="send",
    )(params, send_index, send_count, cameras)


def order_call(tile_lists):
    return pl.pallas_call(
        order_kernel,
        out_shape=(
            pltpu.VMEM((8, slots), jnp.float32),
            pltpu.VMEM((slots, slots), jnp.bfloat16),
        ),
        in_specs=[vector],
        name="order",
    )(near(tile_lists))


def tile_call(arrived, keys, before, tile_pos, target, cameras):
    return pl.pallas_call(
        tile_kernel,
        out_shape=(
            shaped(5, 1, tile_dev * 256),
            pltpu.VMEM((num_view, shards, 128), jnp.float32),
        ),
        in_specs=[vector, vector, vector, scalar, vector, scalar],
        name="tiles",
    )(near(arrived), near(keys), near(before), tile_pos, near(target), cameras)


def update_call(grads, params, adam_m, adam_v, visible):
    return pl.pallas_call(
        functools.partial(update_kernel, 8.0 * (tile_dev * shards) / 64.0),
        out_shape=(shaped(num_param, gauss_dev),) * 3,
        in_specs=[vector] * 5,
        name="update",
    )(near(grads), near(params), near(adam_m), near(adam_v), near(visible))


def body(
    params, adam_m, adam_v, visible, cameras, send_index, send_count, tile_lists, tile_pos, target
):
    sending = send_call(params, send_index, send_count, cameras)
    arrived = lax.all_to_all(sending, "space", split_axis=0, concat_axis=0, tiled=True)
    wanted = jnp.transpose(target, (1, 0, 2))
    keys, before = order_call(tile_lists)
    image, pulled = tile_call(arrived, keys, before, tile_pos, wanted, cameras)
    image = jnp.transpose(image, (1, 0, 2))
    pulled = pulled.reshape(num_view * shards, 128)
    grads = lax.all_to_all(pulled, ("view", "space"), split_axis=0, concat_axis=0, tiled=True)
    grads = grads.reshape(num_view, shards, 128)
    new_params, new_m, new_v = update_call(grads, params, adam_m, adam_v, visible.reshape(8, 128))
    return (image, new_params, new_m, new_v)


def solution(mesh):
    placed = (
        P(None, "space"),
        P(None, "space"),
        P(None, "space"),
        P("space"),
        P("view", None),
        P("view", "space", None),
        P("view", "space", None),
        P("view", "space", None),
        P("view", "space"),
        P("view", None, "space"),
    )
    return jax.shard_map(
        body,
        mesh=mesh,
        in_specs=placed,
        out_specs=(P("view", None, "space"), P(None, "space"), P(None, "space"), P(None, "space")),
        check_vma=False,
    )
```

```python
import functools

import jax
import jax.numpy as jnp
from jax import lax
from jax.experimental import pallas as pl
from jax.experimental.pallas import tpu as pltpu
from jax.sharding import PartitionSpec as P

focal_len = 1000.0
center_x = 512.0
harm_zero = 0.28209479177387814
harm_one = 0.4886025119029199
harm_two = (
    1.0925484305920792,
    -1.0925484305920792,
    0.31539156525252005,
    -1.0925484305920792,
    0.5462742152960396,
)
harm_three = (
    -0.5900435899266435,
    2.890611442640554,
    -0.4570457994644658,
    0.3731763325901154,
    -0.4570457994644658,
    1.445305721320277,
    -0.5900435899266435,
)
beta_one = 0.9
beta_two = 0.99
learn_rate = 0.05
adam_eps = 1e-08
adam_step = 100.0
num_param = 59
num_record = 11
num_view = 4
gauss_dev = 1024
shards = 128
cap = 4
slots = 512
slot_rows = 16
tile_dev = 2
list_len = 512
halves = 2


def project(gauss, camera, center_y):
    rotation = [[camera[3 * i + j] for j in range(3)] for i in range(3)]
    offset = [camera[9 + i] for i in range(3)]
    centre = [gauss[i] for i in range(3)]
    viewed = [sum((rotation[i][j] * centre[j] for j in range(3))) + offset[i] for i in range(3)]
    inverse = 1.0 / viewed[2]
    screen_x = focal_len * viewed[0] * inverse + center_x
    screen_y = focal_len * viewed[1] * inverse + center_y
    scales = [jnp.exp(gauss[3 + i]) for i in range(3)]
    length = jnp.sqrt(
        gauss[6] * gauss[6] + gauss[7] * gauss[7] + gauss[8] * gauss[8] + gauss[9] * gauss[9]
    )
    quat_w, quat_x, quat_y, quat_z = [gauss[6 + i] / length for i in range(4)]
    spin = [
        [
            1.0 - 2.0 * (quat_y * quat_y + quat_z * quat_z),
            2.0 * (quat_x * quat_y - quat_w * quat_z),
            2.0 * (quat_x * quat_z + quat_w * quat_y),
        ],
        [
            2.0 * (quat_x * quat_y + quat_w * quat_z),
            1.0 - 2.0 * (quat_x * quat_x + quat_z * quat_z),
            2.0 * (quat_y * quat_z - quat_w * quat_x),
        ],
        [
            2.0 * (quat_x * quat_z - quat_w * quat_y),
            2.0 * (quat_y * quat_z + quat_w * quat_x),
            1.0 - 2.0 * (quat_x * quat_x + quat_y * quat_y),
        ],
    ]
    factor = [[spin[i][j] * scales[j] for j in range(3)] for i in range(3)]
    sigma = [
        [sum((factor[i][j] * factor[k][j] for j in range(3))) for k in range(3)] for i in range(3)
    ]
    near = focal_len * inverse
    lean_x = -focal_len * viewed[0] * inverse * inverse
    lean_y = -focal_len * viewed[1] * inverse * inverse
    jacob = [
        [near * rotation[0][j] + lean_x * rotation[2][j] for j in range(3)],
        [near * rotation[1][j] + lean_y * rotation[2][j] for j in range(3)],
    ]
    halfway = [
        [sum((jacob[a][i] * sigma[i][k] for i in range(3))) for k in range(3)] for a in range(2)
    ]
    upper = sum((halfway[0][k] * jacob[0][k] for k in range(3))) + 0.3
    middle = sum((halfway[0][k] * jacob[1][k] for k in range(3)))
    lower = sum((halfway[1][k] * jacob[1][k] for k in range(3))) + 0.3
    determinant = upper * lower - middle * middle
    conic_a = lower / determinant
    conic_b = -middle / determinant
    conic_c = upper / determinant
    opacity = jax.nn.sigmoid(gauss[10])
    camera_pos = [-sum((rotation[i][j] * offset[i] for i in range(3))) for j in range(3)]
    toward = [centre[j] - camera_pos[j] for j in range(3)]
    reach = jnp.sqrt(toward[0] * toward[0] + toward[1] * toward[1] + toward[2] * toward[2])
    unit_x = toward[0] / reach
    unit_y = toward[1] / reach
    unit_z = toward[2] / reach
    square_x = unit_x * unit_x
    square_y = unit_y * unit_y
    square_z = unit_z * unit_z
    basis = [
        harm_zero + 0.0 * unit_x,
        -harm_one * unit_y,
        harm_one * unit_z,
        -harm_one * unit_x,
        harm_two[0] * unit_x * unit_y,
        harm_two[1] * unit_y * unit_z,
        harm_two[2] * (2.0 * square_z - square_x - square_y),
        harm_two[3] * unit_x * unit_z,
        harm_two[4] * (square_x - square_y),
        harm_three[0] * unit_y * (3.0 * square_x - square_y),
        harm_three[1] * unit_x * unit_y * unit_z,
        harm_three[2] * unit_y * (4.0 * square_z - square_x - square_y),
        harm_three[3] * unit_z * (2.0 * square_z - 3.0 * square_x - 3.0 * square_y),
        harm_three[4] * unit_x * (4.0 * square_z - square_x - square_y),
        harm_three[5] * unit_z * (square_x - square_y),
        harm_three[6] * unit_x * (square_x - 3.0 * square_y),
    ]
    colors = [0.5 + sum((basis[k] * gauss[11 + 16 * c + k] for k in range(16))) for c in range(3)]
    return [
        screen_x,
        screen_y,
        conic_a,
        conic_b,
        conic_c,
        opacity,
        colors[0],
        colors[1],
        colors[2],
        viewed[2],
        inverse,
    ]


def split_three(values):
    high = values.astype(jnp.bfloat16)
    left = values - high.astype(jnp.float32)
    middle = left.astype(jnp.bfloat16)
    low = (left - middle.astype(jnp.float32)).astype(jnp.bfloat16)
    return high, middle, low


def split_two(values):
    high = values.astype(jnp.bfloat16)
    return high, (values - high.astype(jnp.float32)).astype(jnp.bfloat16)


def contract(left, right, left_dim, right_dim):
    return lax.dot_general(
        left,
        right,
        (((left_dim,), (right_dim,)), ((), ())),
        preferred_element_type=jnp.float32,
    )


def as_mask(condition):
    return jnp.where(condition, jnp.bfloat16(1.0), jnp.bfloat16(0.0))


def short(values):
    return values.astype(jnp.int16)


def write_order(lists, places, key_out, before_out):
    order = jnp.concatenate([lists[0, t : t + 1] for t in range(tile_dev)], axis=1)
    total = tile_dev * list_len
    source = lax.broadcasted_iota(jnp.int32, (shards, total), 0)
    found = as_mask(short(source) == short(order >> 2))
    number = lax.broadcasted_iota(jnp.int32, (8, total), 1) + 1
    row = lax.broadcasted_iota(jnp.int32, (8, total), 0)
    digits = jnp.where(row < 4, number >> 8, number & 255)
    digits = jnp.where((order & 3) == (row & 3), digits, 0).astype(jnp.float32)
    keys = contract(digits.astype(jnp.bfloat16), found, 1, 1)
    keys = 256.0 * keys[0:4] + keys[4:8]
    key = jnp.concatenate([keys[c : c + 1] for c in range(cap)], axis=1)
    key_all = jnp.broadcast_to(key, (8, slots))
    key_col = key_all.T[:, 0:1]
    floor = jnp.where(key > float(list_len), float(list_len), 0.0)
    second = key > float(list_len)
    corner_x = [((places[0, t] & 63) * 16).astype(jnp.float32) + 8.0 for t in range(tile_dev)]
    corner_y = [((places[0, t] >> 6) * 16).astype(jnp.float32) + 8.0 for t in range(tile_dev)]
    key_out[0:1] = key
    key_out[1:2] = jnp.where(second, corner_x[1], corner_x[0])
    key_out[2:3] = jnp.where(second, corner_y[1], corner_y[0])
    key_col, key, floor = [short(part.astype(jnp.int32)) for part in (key_col, key, floor)]
    before_out[...] = as_mask((key_col < key) & (key_col > floor))


def send_kernel(
    center_y, params_in, lists_in, route_in, count_in, camera_in, places_in,
    visible_in, out, key_out, before_out, rows_out, cams_out, visible_out,
    params, lists, route, count, camera, places, turned, sems
):
    sources = (lists_in, route_in, camera_in, params_in, count_in, places_in, visible_in)
    kept = (lists, route, camera, params, count, places, visible_out)
    copies = [
        pltpu.make_async_copy(source, held, sems.at[i])
        for i, (source, held) in enumerate(zip(sources, kept))
    ]
    for copy in copies:
        copy.start()
    copies[0].wait()
    copies[5].wait()
    write_order(lists, places, key_out, before_out)
    copies[1].wait()
    chosen = route[0]
    sub = lax.broadcasted_iota(jnp.int32, (128, slots), 0)
    choose = as_mask(short(sub) == short(chosen & 127))
    copies[2].wait()
    cam = [camera[0, i] for i in range(12)]
    for i in range(12):
        cams_out[i : i + 1] = jnp.full((1, shards), cam[i], jnp.float32)
    copies[3].wait()
    rows = params[...].reshape(num_param, 8, 128)
    rows_out[...] = rows
    records = project([rows[i] for i in range(num_param)], cam, center_y)
    table = jnp.concatenate(split_three(jnp.concatenate(records, axis=0)), axis=0)
    picked = contract(table, choose, 1, 0)
    size = 8 * num_record
    picked = picked[0:size] + (picked[size : 2 * size] + picked[2 * size :])
    high = lax.broadcasted_iota(jnp.int32, (8, slots), 0) == (chosen >> 7)
    sent = [
        jnp.sum(jnp.where(high, picked[8 * r : 8 * r + 8], 0.0), axis=0, keepdims=True)
        for r in range(num_record)
    ]
    sent.append((chosen + 1).astype(jnp.float32))
    sent.append(jnp.zeros((slot_rows - num_record - 1, slots), jnp.float32))
    sent = jnp.concatenate(sent, axis=0)
    turned[:, 0:slot_rows] = sent.T
    parts = [turned[pl.ds(c, shards, stride=cap), :][:, 0:slot_rows] for c in range(cap)]
    width = cap * slot_rows
    spread = jnp.concatenate(parts + [jnp.zeros((shards, 128 - width), jnp.float32)], axis=1)
    copies[4].wait()
    used = jnp.broadcast_to(count[0], (8, shards)).T[:, 0:1]
    lane = lax.broadcasted_iota(jnp.int32, (shards, 128), 1)
    out[...] = jnp.where((lane >> 4) < used, spread, 0.0)
    copies[6].wait()


def tile_kernel(arrived, keys, before_in, target, cams, image_out, out, image, sem):
    turned = arrived[...].T
    rec = jnp.concatenate([turned[c * slot_rows : (c + 1) * slot_rows] for c in range(cap)], axis=1)
    key = keys[0:1]
    second = key > float(list_len)
    before = before_in[...]
    at_x = rec[0:1] - keys[1:2]
    at_y = rec[1:2] - keys[2:3]
    con_a, con_b, con_c = rec[2:3], rec[3:4], rec[4:5]
    half_a, half_c = -0.5 * con_a, -0.5 * con_c
    opacity = jnp.where(key > 0.0, rec[5:6], 0.0)
    feats = rec[6:11]
    gap = jnp.zeros((3, slots), jnp.float32)
    feats = jnp.concatenate(
        [jnp.where(second, 0.0, feats), gap, jnp.where(second, feats, 0.0), gap], axis=0
    )
    f_hi, f_lo, f_last = split_three(feats)
    f_both = jnp.concatenate([f_hi, f_lo], axis=0)
    f_six = jnp.concatenate([f_hi, f_lo, f_hi, f_lo, f_last, f_hi], axis=0)
    size = 256 // halves
    rows = range(halves)
    seat = lax.broadcasted_iota(jnp.int32, (8, size), 1)
    row = lax.broadcasted_iota(jnp.int32, (8, size), 0)
    seat_x = (seat & 15).astype(jnp.float32) - 7.5
    gap = jnp.zeros((3, size), jnp.float32)

    side = lax.broadcasted_iota(jnp.int32, (16, 1), 0).astype(jnp.float32) - 7.5
    scale = 1.4426950408889634
    apart_x = side - at_x
    slope_x = (scale * half_a) * apart_x
    apart_y = side - at_y
    slope_y = (scale * con_b) * apart_y
    bend_y = (scale * half_c) * apart_y * apart_y

    def shade(i):
        power = [
            apart_x * (slope_x - slope_y[y : y + 1]) + bend_y[y : y + 1]
            for y in range(i * size // 16, (i + 1) * size // 16)
        ]
        alpha = opacity * jnp.exp2(jnp.concatenate(power, axis=0))
        keep = 1.0 - alpha
        return alpha, keep, jnp.concatenate(split_two(jnp.log(keep)), axis=0)

    def blend(i, alpha, logs):
        sums = contract(logs, before, 1, 0)
        through = jnp.exp(sums[0:size] + sums[size:])
        weight = alpha * through
        return weight, split_two(weight)

    def draw(i, w_hi, w_lo):
        drawn = contract(f_both, w_hi, 1, 1)
        drawn = drawn[0:16] + (drawn[16:32] + contract(f_hi, w_lo, 1, 1))
        parts = []
        for t in range(tile_dev):
            shown = drawn[8 * t : 8 * t + 5]
            spot = pl.ds(t * 256 + i * size, size)
            for ch in range(5):
                image[ch, :, spot] = shown[ch : ch + 1]
            wanted = jnp.concatenate([target[ch, :, spot] for ch in range(5)], axis=0)
            parts += [shown - wanted, gap]
        return split_three(jnp.concatenate(parts, axis=0))

    def score_of(g_hi, g_lo, g_last, weight):
        score = contract(
            jnp.concatenate([g_hi, g_hi, g_lo, g_lo, g_hi, g_last], axis=0), f_six, 0, 0
        )
        gain = weight * score
        return gain, jnp.concatenate(split_two(gain), axis=0)

    def pull_of(ratio, gain, tails):
        tail = contract(tails, before, 1, 1)
        tail = tail[0:size] + tail[size:]
        return jnp.concatenate(split_three(gain - ratio * tail), axis=0)

    def moments_of(i, pull):
        seat_y = (seat >> 4).astype(jnp.float32) + (i * size // 16 - 7.5)
        first = jnp.where((row == 1) | (row == 3) | (row == 4), seat_x, 1.0)
        first = jnp.where((row == 2) | (row == 5), seat_y, first)
        other = jnp.where(row == 3, seat_x, 1.0)
        other = jnp.where((row == 4) | (row == 5), seat_y, other)
        basis = (first * other).astype(jnp.bfloat16)
        return contract(jnp.concatenate([basis] * 3, axis=1), pull, 1, 0)

    def colors_of(g_hi, g_lo, g_last, w_hi, w_lo):
        color = contract(jnp.concatenate([g_hi, g_lo], axis=0), w_hi, 1, 0)
        return color[0:16] + (color[16:32] + contract(g_hi, w_lo, 1, 0))

    shaded = [shade(i) for i in rows]
    blended = [blend(i, shaded[i][0], shaded[i][2]) for i in rows]
    diffs = [draw(i, *blended[i][1]) for i in rows]
    shown = pltpu.make_async_copy(image, image_out, sem)
    shown.start()
    scores = [score_of(*diffs[i], blended[i][0]) for i in rows]
    color = sum(colors_of(*diffs[i], *blended[i][1]) for i in rows)
    pulls = [
        pull_of(shaded[i][0] / shaded[i][1], *scores[i]) for i in rows
    ]
    moments = sum(moments_of(i, pulls[i]) for i in rows)
    m_0, m_x, m_y, m_xx, m_xy, m_yy = [moments[i : i + 1] for i in range(6)]
    d_x = m_x - at_x * m_0
    d_y = m_y - at_y * m_0
    d_xx = m_xx - at_x * (m_x + d_x)
    d_xy = m_xy - at_x * m_y - at_y * d_x
    d_yy = m_yy - at_y * (m_y + d_y)
    color = jnp.where(second, color[8:13], color[0:5])
    pulled = jnp.concatenate(
        [
            con_a * d_x + con_b * d_y,
            con_b * d_x + con_c * d_y,
            -0.5 * d_xx,
            -d_xy,
            -0.5 * d_yy,
            jnp.where(opacity > 0.0, m_0 / jnp.where(opacity > 0.0, opacity, 1.0), 0.0),
            color,
            rec[11:12],
            jnp.zeros((4, slots), jnp.float32),
        ],
        axis=0,
    )
    stacked = [pulled[:, c * shards : (c + 1) * shards] for c in range(cap)]
    stacked.append(cams[...])
    stacked.append(jnp.zeros((128 - cap * slot_rows - 12, shards), jnp.float32))
    block = jnp.concatenate(stacked, axis=0).T
    for w in range(num_view):
        out[w] = block
    shown.wait()


def update_kernel(center_y, grads, rows, params, adam_m, adam_v, visible, new_p, new_m, new_v):
    turned = [grads[w].T for w in range(num_view)]
    slot = [turned[w][c * slot_rows : (c + 1) * slot_rows] for w in range(num_view) for c in range(cap)]
    slot = jnp.concatenate(slot, axis=1)
    total = num_view * slots
    number = slot[num_record : num_record + 1].astype(jnp.int32) - 1
    viewer = (lax.broadcasted_iota(jnp.int32, (1, total), 1) >> 9).astype(jnp.float32) + 1.0
    high = lax.broadcasted_iota(jnp.int32, (8, total), 0) == (number >> 7)
    place = as_mask(
        short(lax.broadcasted_iota(jnp.int32, (128, total), 0)) == short(number & 127)
    )
    coarse = slot.astype(jnp.bfloat16).astype(jnp.float32)
    fine = slot - coarse
    spread = [jnp.where(high, coarse[r : r + 1], 0.0) for r in range(num_record)]
    spread.append(jnp.where(high, viewer, 0.0))
    spread += [jnp.where(high, fine[r : r + 1], 0.0) for r in range(num_record)]
    placed = contract(jnp.concatenate(spread, axis=0).astype(jnp.bfloat16), place, 1, 1)
    size = 8 * num_record
    seen = placed[size : size + 8]
    placed = placed[0:size] + placed[size + 8 :]
    pulled = [placed[8 * r : 8 * r + 8] for r in range(num_record)]
    base = cap * slot_rows
    cam = []
    for i in range(12):
        value = jnp.broadcast_to(turned[0][base + i : base + i + 1], (8, 128))
        for w in range(1, num_view):
            value = jnp.where(seen == w + 1.0, turned[w][base + i : base + i + 1], value)
        cam.append(value)
    _, pull = jax.vjp(
        lambda *gauss: project(gauss, cam, center_y), *[rows[i] for i in range(num_param)]
    )
    grad = jnp.stack(pull(pulled)).reshape(num_param, gauss_dev)
    keep = jnp.broadcast_to(visible[...].reshape(1, gauss_dev) > 0, grad.shape)
    old, old_m, old_v = params[...], adam_m[...], adam_v[...]
    moment_one = beta_one * old_m + (1.0 - beta_one) * grad
    moment_two = beta_two * old_v + (1.0 - beta_two) * grad * grad
    step = moment_one * (learn_rate / (1.0 - beta_one**adam_step))
    second_hat = moment_two * (1.0 / (1.0 - beta_two**adam_step))
    stepped = old - step / (jnp.sqrt(second_hat) + adam_eps)
    new_p[...] = jnp.where(keep, stepped, old)
    new_m[...] = jnp.where(keep, moment_one, old_m)
    new_v[...] = jnp.where(keep, moment_two, old_v)


def shaped(*dims):
    return jax.ShapeDtypeStruct(dims, jnp.float32)


def near(array):
    return pltpu.with_memory_space_constraint(array, pltpu.VMEM)


vector = pl.BlockSpec(memory_space=pltpu.VMEM)
scalar = pl.BlockSpec(memory_space=pltpu.SMEM)


def send_call(params, tile_lists, send_index, send_count, cameras, tile_pos, visible):
    return pl.pallas_call(
        functools.partial(send_kernel, 8.0 * (tile_dev * shards) / 64.0),
        out_shape=(
            pltpu.VMEM((shards, 128), jnp.float32),
            pltpu.VMEM((8, slots), jnp.float32),
            pltpu.VMEM((slots, slots), jnp.bfloat16),
            pltpu.VMEM((num_param, 8, 128), jnp.float32),
            pltpu.VMEM((12, shards), jnp.float32),
            pltpu.VMEM((8, 128), jnp.int32),
        ),
        in_specs=[pl.BlockSpec(memory_space=pl.ANY)] * 7,
        scratch_shapes=[
            pltpu.VMEM((num_param, gauss_dev), jnp.float32),
            pltpu.VMEM((1, tile_dev, list_len), jnp.int32),
            pltpu.VMEM((1, 1, slots), jnp.int32),
            pltpu.VMEM((1, 1, shards), jnp.int32),
            pltpu.SMEM((1, 12), jnp.float32),
            pltpu.SMEM((1, tile_dev), jnp.int32),
            pltpu.VMEM((slots, 128), jnp.float32),
            pltpu.SemaphoreType.DMA((7,)),
        ],
        name="send",
    )(params, tile_lists, send_index, send_count, cameras, tile_pos, visible)


def tile_call(arrived, keys, before, target, cams):
    return pl.pallas_call(
        tile_kernel,
        out_shape=(
            shaped(5, 1, tile_dev * 256),
            pltpu.VMEM((num_view, shards, 128), jnp.float32),
        ),
        in_specs=[vector] * 5,
        out_specs=[pl.BlockSpec(memory_space=pl.ANY), vector],
        scratch_shapes=[
            pltpu.VMEM((5, 1, tile_dev * 256), jnp.float32),
            pltpu.SemaphoreType.DMA,
        ],
        name="tiles",
    )(near(arrived), near(keys), near(before), near(target), near(cams))


def update_call(grads, rows, params, adam_m, adam_v, visible):
    return pl.pallas_call(
        functools.partial(update_kernel, 8.0 * (tile_dev * shards) / 64.0),
        out_shape=(shaped(num_param, gauss_dev),) * 3,
        in_specs=[vector] * 6,
        name="update",
    )(near(grads), near(rows), near(params), near(adam_m), near(adam_v), near(visible))


def body(
    params, adam_m, adam_v, visible, cameras, send_index, send_count, tile_lists, tile_pos, target
):
    sending, keys, before, rows, cams, shown = send_call(
        params, tile_lists, send_index, send_count, cameras, tile_pos, visible.reshape(8, 128)
    )
    arrived = lax.all_to_all(sending, "space", split_axis=0, concat_axis=0, tiled=True)
    wanted = jnp.transpose(target, (1, 0, 2))
    image, pulled = tile_call(arrived, keys, before, wanted, cams)
    image = jnp.transpose(image, (1, 0, 2))
    pulled = pulled.reshape(num_view * shards, 128)
    grads = lax.all_to_all(pulled, ("view", "space"), split_axis=0, concat_axis=0, tiled=True)
    grads = grads.reshape(num_view, shards, 128)
    new_params, new_m, new_v = update_call(grads, rows, params, adam_m, adam_v, shown)
    return (image, new_params, new_m, new_v)


def solution(mesh):
    placed = (
        P(None, "space"),
        P(None, "space"),
        P(None, "space"),
        P("space"),
        P("view", None),
        P("view", "space", None),
        P("view", "space", None),
        P("view", "space", None),
        P("view", "space"),
        P("view", None, "space"),
    )
    return jax.shard_map(
        body,
        mesh=mesh,
        in_specs=placed,
        out_specs=(P("view", None, "space"), P(None, "space"), P(None, "space"), P(None, "space")),
        check_vma=False,
    )
```

```python
import functools

import jax
import jax.numpy as jnp
from jax import lax
from jax.experimental import pallas as pl
from jax.experimental.pallas import tpu as pltpu
from jax.sharding import PartitionSpec as P

focal_len = 1000.0
center_x = 512.0
harm_zero = 0.28209479177387814
harm_one = 0.4886025119029199
harm_two = (
    1.0925484305920792,
    -1.0925484305920792,
    0.31539156525252005,
    -1.0925484305920792,
    0.5462742152960396,
)
harm_three = (
    -0.5900435899266435,
    2.890611442640554,
    -0.4570457994644658,
    0.3731763325901154,
    -0.4570457994644658,
    1.445305721320277,
    -0.5900435899266435,
)
beta_one = 0.9
beta_two = 0.99
learn_rate = 0.05
adam_eps = 1e-08
adam_step = 100.0
num_param = 59
num_record = 11
num_view = 4
gauss_dev = 1024
shards = 128
cap = 4
slots = 512
slot_rows = 16
tile_dev = 2
list_len = 512
halves = 2


def project(gauss, camera, center_y):
    rotation = [[camera[3 * i + j] for j in range(3)] for i in range(3)]
    offset = [camera[9 + i] for i in range(3)]
    centre = [gauss[i] for i in range(3)]
    viewed = [sum((rotation[i][j] * centre[j] for j in range(3))) + offset[i] for i in range(3)]
    inverse = 1.0 / viewed[2]
    screen_x = focal_len * viewed[0] * inverse + center_x
    screen_y = focal_len * viewed[1] * inverse + center_y
    scales = [jnp.exp(gauss[3 + i]) for i in range(3)]
    length = jnp.sqrt(
        gauss[6] * gauss[6] + gauss[7] * gauss[7] + gauss[8] * gauss[8] + gauss[9] * gauss[9]
    )
    quat_w, quat_x, quat_y, quat_z = [gauss[6 + i] / length for i in range(4)]
    spin = [
        [
            1.0 - 2.0 * (quat_y * quat_y + quat_z * quat_z),
            2.0 * (quat_x * quat_y - quat_w * quat_z),
            2.0 * (quat_x * quat_z + quat_w * quat_y),
        ],
        [
            2.0 * (quat_x * quat_y + quat_w * quat_z),
            1.0 - 2.0 * (quat_x * quat_x + quat_z * quat_z),
            2.0 * (quat_y * quat_z - quat_w * quat_x),
        ],
        [
            2.0 * (quat_x * quat_z - quat_w * quat_y),
            2.0 * (quat_y * quat_z + quat_w * quat_x),
            1.0 - 2.0 * (quat_x * quat_x + quat_y * quat_y),
        ],
    ]
    factor = [[spin[i][j] * scales[j] for j in range(3)] for i in range(3)]
    sigma = [
        [sum((factor[i][j] * factor[k][j] for j in range(3))) for k in range(3)] for i in range(3)
    ]
    near = focal_len * inverse
    lean_x = -focal_len * viewed[0] * inverse * inverse
    lean_y = -focal_len * viewed[1] * inverse * inverse
    jacob = [
        [near * rotation[0][j] + lean_x * rotation[2][j] for j in range(3)],
        [near * rotation[1][j] + lean_y * rotation[2][j] for j in range(3)],
    ]
    halfway = [
        [sum((jacob[a][i] * sigma[i][k] for i in range(3))) for k in range(3)] for a in range(2)
    ]
    upper = sum((halfway[0][k] * jacob[0][k] for k in range(3))) + 0.3
    middle = sum((halfway[0][k] * jacob[1][k] for k in range(3)))
    lower = sum((halfway[1][k] * jacob[1][k] for k in range(3))) + 0.3
    determinant = upper * lower - middle * middle
    conic_a = lower / determinant
    conic_b = -middle / determinant
    conic_c = upper / determinant
    opacity = jax.nn.sigmoid(gauss[10])
    camera_pos = [-sum((rotation[i][j] * offset[i] for i in range(3))) for j in range(3)]
    toward = [centre[j] - camera_pos[j] for j in range(3)]
    reach = jnp.sqrt(toward[0] * toward[0] + toward[1] * toward[1] + toward[2] * toward[2])
    unit_x = toward[0] / reach
    unit_y = toward[1] / reach
    unit_z = toward[2] / reach
    square_x = unit_x * unit_x
    square_y = unit_y * unit_y
    square_z = unit_z * unit_z
    basis = [
        harm_zero + 0.0 * unit_x,
        -harm_one * unit_y,
        harm_one * unit_z,
        -harm_one * unit_x,
        harm_two[0] * unit_x * unit_y,
        harm_two[1] * unit_y * unit_z,
        harm_two[2] * (2.0 * square_z - square_x - square_y),
        harm_two[3] * unit_x * unit_z,
        harm_two[4] * (square_x - square_y),
        harm_three[0] * unit_y * (3.0 * square_x - square_y),
        harm_three[1] * unit_x * unit_y * unit_z,
        harm_three[2] * unit_y * (4.0 * square_z - square_x - square_y),
        harm_three[3] * unit_z * (2.0 * square_z - 3.0 * square_x - 3.0 * square_y),
        harm_three[4] * unit_x * (4.0 * square_z - square_x - square_y),
        harm_three[5] * unit_z * (square_x - square_y),
        harm_three[6] * unit_x * (square_x - 3.0 * square_y),
    ]
    colors = [0.5 + sum((basis[k] * gauss[11 + 16 * c + k] for k in range(16))) for c in range(3)]
    return [
        screen_x,
        screen_y,
        conic_a,
        conic_b,
        conic_c,
        opacity,
        colors[0],
        colors[1],
        colors[2],
        viewed[2],
        inverse,
    ]


def split_three(values):
    high = values.astype(jnp.bfloat16)
    left = values - high.astype(jnp.float32)
    middle = left.astype(jnp.bfloat16)
    low = (left - middle.astype(jnp.float32)).astype(jnp.bfloat16)
    return high, middle, low


def split_two(values):
    high = values.astype(jnp.bfloat16)
    return high, (values - high.astype(jnp.float32)).astype(jnp.bfloat16)


def contract(left, right, left_dim, right_dim):
    return lax.dot_general(
        left,
        right,
        (((left_dim,), (right_dim,)), ((), ())),
        preferred_element_type=jnp.float32,
    )


def as_mask(condition):
    return jnp.where(condition, jnp.bfloat16(1.0), jnp.bfloat16(0.0))


def short(values):
    return values.astype(jnp.int16)


def write_order(lists, places, key_out, before_out):
    order = jnp.concatenate([lists[0, t : t + 1] for t in range(tile_dev)], axis=1)
    total = tile_dev * list_len
    source = lax.broadcasted_iota(jnp.int32, (shards, total), 0)
    found = as_mask(short(source) == short(order >> 2))
    number = lax.broadcasted_iota(jnp.int32, (8, total), 1) + 1
    row = lax.broadcasted_iota(jnp.int32, (8, total), 0)
    digits = jnp.where(row < 4, number >> 8, number & 255)
    digits = jnp.where((order & 3) == (row & 3), digits, 0).astype(jnp.float32)
    keys = contract(digits.astype(jnp.bfloat16), found, 1, 1)
    keys = 256.0 * keys[0:4] + keys[4:8]
    key = jnp.concatenate([keys[c : c + 1] for c in range(cap)], axis=1)
    key_all = jnp.broadcast_to(key, (8, slots))
    key_col = key_all.T[:, 0:1]
    floor = jnp.where(key > float(list_len), float(list_len), 0.0)
    second = key > float(list_len)
    corner_x = [((places[0, t] & 63) * 16).astype(jnp.float32) + 8.0 for t in range(tile_dev)]
    corner_y = [((places[0, t] >> 6) * 16).astype(jnp.float32) + 8.0 for t in range(tile_dev)]
    key_out[0:1] = key
    key_out[1:2] = jnp.where(second, corner_x[1], corner_x[0])
    key_out[2:3] = jnp.where(second, corner_y[1], corner_y[0])
    key_col, key, floor = [short(part.astype(jnp.int32)) for part in (key_col, key, floor)]
    before_out[...] = as_mask((key_col < key) & (key_col > floor))


def send_kernel(
    center_y, params_in, lists_in, route_in, count_in, camera_in, places_in,
    visible_in, out, key_out, before_out, rows_out, cams_out, visible_out,
    params, lists, route, count, camera, places, turned, sems
):
    sources = (lists_in, route_in, camera_in, params_in, count_in, places_in, visible_in)
    kept = (lists, route, camera, params, count, places, visible_out)
    copies = [
        pltpu.make_async_copy(source, held, sems.at[i])
        for i, (source, held) in enumerate(zip(sources, kept))
    ]
    for copy in copies:
        copy.start()
    copies[0].wait()
    copies[5].wait()
    write_order(lists, places, key_out, before_out)
    copies[1].wait()
    chosen = route[0]
    sub = lax.broadcasted_iota(jnp.int32, (128, slots), 0)
    choose = as_mask(short(sub) == short(chosen & 127))
    copies[2].wait()
    cam = [camera[0, i] for i in range(12)]
    for i in range(12):
        cams_out[i : i + 1] = jnp.full((1, shards), cam[i], jnp.float32)
    copies[3].wait()
    rows = params[...].reshape(num_param, 8, 128)
    rows_out[...] = rows
    records = project([rows[i] for i in range(num_param)], cam, center_y)
    table = jnp.concatenate(split_three(jnp.concatenate(records, axis=0)), axis=0)
    picked = contract(table, choose, 1, 0)
    size = 8 * num_record
    picked = picked[0:size] + (picked[size : 2 * size] + picked[2 * size :])
    high = lax.broadcasted_iota(jnp.int32, (8, slots), 0) == (chosen >> 7)
    sent = [
        jnp.sum(jnp.where(high, picked[8 * r : 8 * r + 8], 0.0), axis=0, keepdims=True)
        for r in range(num_record)
    ]
    sent.append((chosen + 1).astype(jnp.float32))
    sent.append(jnp.zeros((slot_rows - num_record - 1, slots), jnp.float32))
    sent = jnp.concatenate(sent, axis=0)
    turned[:, 0:slot_rows] = sent.T
    parts = [turned[pl.ds(c, shards, stride=cap), :][:, 0:slot_rows] for c in range(cap)]
    width = cap * slot_rows
    spread = jnp.concatenate(parts + [jnp.zeros((shards, 128 - width), jnp.float32)], axis=1)
    copies[4].wait()
    used = jnp.broadcast_to(count[0], (8, shards)).T[:, 0:1]
    lane = lax.broadcasted_iota(jnp.int32, (shards, 128), 1)
    out[...] = jnp.where((lane >> 4) < used, spread, 0.0)
    copies[6].wait()


def tile_kernel(arrived, keys, before_in, target, cams, image_out, out, image, sem):
    turned = arrived[...].T
    rec = jnp.concatenate([turned[c * slot_rows : (c + 1) * slot_rows] for c in range(cap)], axis=1)
    key = keys[0:1]
    second = key > float(list_len)
    before = before_in[...]
    at_x = rec[0:1] - keys[1:2]
    at_y = rec[1:2] - keys[2:3]
    con_a, con_b, con_c = rec[2:3], rec[3:4], rec[4:5]
    half_a, half_c = -0.5 * con_a, -0.5 * con_c
    opacity = jnp.where(key > 0.0, rec[5:6], 0.0)
    feats = rec[6:11]
    gap = jnp.zeros((3, slots), jnp.float32)
    feats = jnp.concatenate(
        [jnp.where(second, 0.0, feats), gap, jnp.where(second, feats, 0.0), gap], axis=0
    )
    f_hi, f_lo, f_last = split_three(feats)
    f_both = jnp.concatenate([f_hi, f_lo], axis=0)
    f_six = jnp.concatenate([f_hi, f_lo, f_hi, f_lo, f_last, f_hi], axis=0)
    size = 256 // halves
    rows = range(halves)
    seat = lax.broadcasted_iota(jnp.int32, (8, size), 1)
    row = lax.broadcasted_iota(jnp.int32, (8, size), 0)
    seat_x = (seat & 15).astype(jnp.float32) - 7.5
    gap = jnp.zeros((3, size), jnp.float32)

    side = lax.broadcasted_iota(jnp.int32, (16, 1), 0).astype(jnp.float32) - 7.5
    scale = 1.4426950408889634
    apart_x = side - at_x
    slope_x = (scale * half_a) * apart_x
    apart_y = side - at_y
    slope_y = (scale * con_b) * apart_y
    bend_y = (scale * half_c) * apart_y * apart_y

    def shade(i):
        power = [
            apart_x * (slope_x - slope_y[y : y + 1]) + bend_y[y : y + 1]
            for y in range(i * size // 16, (i + 1) * size // 16)
        ]
        alpha = opacity * jnp.exp2(jnp.concatenate(power, axis=0))
        keep = 1.0 - alpha
        return alpha, keep, jnp.concatenate(split_two(jnp.log(keep)), axis=0)

    def blend(i, alpha, logs):
        sums = contract(logs, before, 1, 0)
        through = jnp.exp(sums[0:size] + sums[size:])
        weight = alpha * through
        return weight, split_two(weight)

    def draw(i, w_hi, w_lo):
        drawn = contract(f_both, w_hi, 1, 1)
        drawn = drawn[0:16] + (drawn[16:32] + contract(f_hi, w_lo, 1, 1))
        parts = []
        for t in range(tile_dev):
            shown = drawn[8 * t : 8 * t + 5]
            spot = pl.ds(t * 256 + i * size, size)
            for ch in range(5):
                image[ch, :, spot] = shown[ch : ch + 1]
            wanted = jnp.concatenate([target[ch, :, spot] for ch in range(5)], axis=0)
            parts += [shown - wanted, gap]
        return split_three(jnp.concatenate(parts, axis=0))

    def score_of(g_hi, g_lo, g_last, weight):
        score = contract(
            jnp.concatenate([g_hi, g_hi, g_lo, g_lo, g_hi, g_last], axis=0), f_six, 0, 0
        )
        gain = weight * score
        return gain, jnp.concatenate(split_two(gain), axis=0)

    def pull_of(ratio, gain, tails):
        tail = contract(tails, before, 1, 1)
        tail = tail[0:size] + tail[size:]
        return jnp.concatenate(split_three(gain - ratio * tail), axis=0)

    def moments_of(i, pull):
        seat_y = (seat >> 4).astype(jnp.float32) + (i * size // 16 - 7.5)
        first = jnp.where((row == 1) | (row == 3) | (row == 4), seat_x, 1.0)
        first = jnp.where((row == 2) | (row == 5), seat_y, first)
        other = jnp.where(row == 3, seat_x, 1.0)
        other = jnp.where((row == 4) | (row == 5), seat_y, other)
        basis = (first * other).astype(jnp.bfloat16)
        return contract(jnp.concatenate([basis] * 3, axis=1), pull, 1, 0)

    def colors_of(g_hi, g_lo, g_last, w_hi, w_lo):
        color = contract(jnp.concatenate([g_hi, g_lo], axis=0), w_hi, 1, 0)
        return color[0:16] + (color[16:32] + contract(g_hi, w_lo, 1, 0))

    shaded = [shade(i) for i in rows]
    blended = [blend(i, shaded[i][0], shaded[i][2]) for i in rows]
    diffs = [draw(i, *blended[i][1]) for i in rows]
    shown = pltpu.make_async_copy(image, image_out, sem)
    shown.start()
    scores = [score_of(*diffs[i], blended[i][0]) for i in rows]
    color = sum(colors_of(*diffs[i], *blended[i][1]) for i in rows)
    pulls = [
        pull_of(shaded[i][0] / shaded[i][1], *scores[i]) for i in rows
    ]
    moments = sum(moments_of(i, pulls[i]) for i in rows)
    m_0, m_x, m_y, m_xx, m_xy, m_yy = [moments[i : i + 1] for i in range(6)]
    d_x = m_x - at_x * m_0
    d_y = m_y - at_y * m_0
    d_xx = m_xx - at_x * (m_x + d_x)
    d_xy = m_xy - at_x * m_y - at_y * d_x
    d_yy = m_yy - at_y * (m_y + d_y)
    color = jnp.where(second, color[8:13], color[0:5])
    pulled = jnp.concatenate(
        [
            con_a * d_x + con_b * d_y,
            con_b * d_x + con_c * d_y,
            -0.5 * d_xx,
            -d_xy,
            -0.5 * d_yy,
            jnp.where(opacity > 0.0, m_0 / jnp.where(opacity > 0.0, opacity, 1.0), 0.0),
            color,
            rec[11:12],
            jnp.zeros((4, slots), jnp.float32),
        ],
        axis=0,
    )
    stacked = [pulled[:, c * shards : (c + 1) * shards] for c in range(cap)]
    stacked.append(cams[...])
    stacked.append(jnp.zeros((128 - cap * slot_rows - 12, shards), jnp.float32))
    block = jnp.concatenate(stacked, axis=0).T
    out[...] = block
    shown.wait()


def update_kernel(center_y, grads, rows, params, adam_m, adam_v, visible, new_p, new_m, new_v):
    turned = [grads[w].T for w in range(num_view)]
    slot = [turned[w][c * slot_rows : (c + 1) * slot_rows] for w in range(num_view) for c in range(cap)]
    slot = jnp.concatenate(slot, axis=1)
    total = num_view * slots
    number = slot[num_record : num_record + 1].astype(jnp.int32) - 1
    viewer = (lax.broadcasted_iota(jnp.int32, (1, total), 1) >> 9).astype(jnp.float32) + 1.0
    high = lax.broadcasted_iota(jnp.int32, (8, total), 0) == (number >> 7)
    place = as_mask(
        short(lax.broadcasted_iota(jnp.int32, (128, total), 0)) == short(number & 127)
    )
    coarse = slot.astype(jnp.bfloat16).astype(jnp.float32)
    fine = slot - coarse
    spread = [jnp.where(high, coarse[r : r + 1], 0.0) for r in range(num_record)]
    spread.append(jnp.where(high, viewer, 0.0))
    spread += [jnp.where(high, fine[r : r + 1], 0.0) for r in range(num_record)]
    placed = contract(jnp.concatenate(spread, axis=0).astype(jnp.bfloat16), place, 1, 1)
    size = 8 * num_record
    seen = placed[size : size + 8]
    placed = placed[0:size] + placed[size + 8 :]
    pulled = [placed[8 * r : 8 * r + 8] for r in range(num_record)]
    base = cap * slot_rows
    cam = []
    for i in range(12):
        value = jnp.broadcast_to(turned[0][base + i : base + i + 1], (8, 128))
        for w in range(1, num_view):
            value = jnp.where(seen == w + 1.0, turned[w][base + i : base + i + 1], value)
        cam.append(value)
    _, pull = jax.vjp(
        lambda *gauss: project(gauss, cam, center_y), *[rows[i] for i in range(num_param)]
    )
    grad = jnp.stack(pull(pulled)).reshape(num_param, gauss_dev)
    keep = jnp.where(visible[...].reshape(1, gauss_dev) > 0, 1.0, 0.0)
    rate_one = (1.0 - beta_one) * keep
    rate_two = (1.0 - beta_two) * keep
    rate = (learn_rate / (1.0 - beta_one**adam_step)) * keep
    old, old_m, old_v = params[...], adam_m[...], adam_v[...]
    moment_one = old_m + rate_one * (grad - old_m)
    moment_two = old_v + rate_two * (grad * grad - old_v)
    second_hat = moment_two * (1.0 / (1.0 - beta_two**adam_step))
    new_p[...] = old - rate * moment_one / (jnp.sqrt(second_hat) + adam_eps)
    new_m[...] = moment_one
    new_v[...] = moment_two


def shaped(*dims):
    return jax.ShapeDtypeStruct(dims, jnp.float32)


def near(array):
    return pltpu.with_memory_space_constraint(array, pltpu.VMEM)


vector = pl.BlockSpec(memory_space=pltpu.VMEM)
scalar = pl.BlockSpec(memory_space=pltpu.SMEM)


def send_call(params, tile_lists, send_index, send_count, cameras, tile_pos, visible):
    return pl.pallas_call(
        functools.partial(send_kernel, 8.0 * (tile_dev * shards) / 64.0),
        out_shape=(
            pltpu.VMEM((shards, 128), jnp.float32),
            pltpu.VMEM((8, slots), jnp.float32),
            pltpu.VMEM((slots, slots), jnp.bfloat16),
            pltpu.VMEM((num_param, 8, 128), jnp.float32),
            pltpu.VMEM((12, shards), jnp.float32),
            pltpu.VMEM((8, 128), jnp.int32),
        ),
        in_specs=[pl.BlockSpec(memory_space=pl.ANY)] * 7,
        scratch_shapes=[
            pltpu.VMEM((num_param, gauss_dev), jnp.float32),
            pltpu.VMEM((1, tile_dev, list_len), jnp.int32),
            pltpu.VMEM((1, 1, slots), jnp.int32),
            pltpu.VMEM((1, 1, shards), jnp.int32),
            pltpu.SMEM((1, 12), jnp.float32),
            pltpu.SMEM((1, tile_dev), jnp.int32),
            pltpu.VMEM((slots, 128), jnp.float32),
            pltpu.SemaphoreType.DMA((7,)),
        ],
        name="send",
    )(params, tile_lists, send_index, send_count, cameras, tile_pos, visible)


def tile_call(arrived, keys, before, target, cams):
    return pl.pallas_call(
        tile_kernel,
        out_shape=(
            shaped(5, 1, tile_dev * 256),
            pltpu.VMEM((shards, 128), jnp.float32),
        ),
        in_specs=[vector] * 5,
        out_specs=[pl.BlockSpec(memory_space=pl.ANY), vector],
        scratch_shapes=[
            pltpu.VMEM((5, 1, tile_dev * 256), jnp.float32),
            pltpu.SemaphoreType.DMA,
        ],
        name="tiles",
    )(near(arrived), near(keys), near(before), near(target), near(cams))


def update_call(grads, rows, params, adam_m, adam_v, visible):
    return pl.pallas_call(
        functools.partial(update_kernel, 8.0 * (tile_dev * shards) / 64.0),
        out_shape=(shaped(num_param, gauss_dev),) * 3,
        in_specs=[vector] * 6,
        name="update",
    )(near(grads), near(rows), near(params), near(adam_m), near(adam_v), near(visible))


def body(
    params, adam_m, adam_v, visible, cameras, send_index, send_count, tile_lists, tile_pos, target
):
    sending, keys, before, rows, cams, shown = send_call(
        params, tile_lists, send_index, send_count, cameras, tile_pos, visible.reshape(8, 128)
    )
    arrived = lax.all_to_all(sending, "space", split_axis=0, concat_axis=0, tiled=True)
    wanted = jnp.transpose(target, (1, 0, 2))
    image, pulled = tile_call(arrived, keys, before, wanted, cams)
    image = jnp.transpose(image, (1, 0, 2))
    pulled = lax.all_to_all(pulled, "space", split_axis=0, concat_axis=0, tiled=True)
    pulled = jnp.broadcast_to(pulled[None], (num_view, shards, 128))
    grads = lax.all_to_all(pulled, "view", split_axis=0, concat_axis=0, tiled=True)
    new_params, new_m, new_v = update_call(grads, rows, params, adam_m, adam_v, shown)
    return (image, new_params, new_m, new_v)


def solution(mesh):
    placed = (
        P(None, "space"),
        P(None, "space"),
        P(None, "space"),
        P("space"),
        P("view", None),
        P("view", "space", None),
        P("view", "space", None),
        P("view", "space", None),
        P("view", "space"),
        P("view", None, "space"),
    )
    return jax.shard_map(
        body,
        mesh=mesh,
        in_specs=placed,
        out_specs=(P("view", None, "space"), P(None, "space"), P(None, "space"), P(None, "space")),
        check_vma=False,
    )
```

```python
import functools

import jax
import jax.numpy as jnp
from jax import lax
from jax.experimental import pallas as pl
from jax.experimental.pallas import tpu as pltpu
from jax.sharding import PartitionSpec as P

focal_len = 1000.0
center_x = 512.0
harm_zero = 0.28209479177387814
harm_one = 0.4886025119029199
harm_two = (
    1.0925484305920792,
    -1.0925484305920792,
    0.31539156525252005,
    -1.0925484305920792,
    0.5462742152960396,
)
harm_three = (
    -0.5900435899266435,
    2.890611442640554,
    -0.4570457994644658,
    0.3731763325901154,
    -0.4570457994644658,
    1.445305721320277,
    -0.5900435899266435,
)
beta_one = 0.9
beta_two = 0.99
learn_rate = 0.05
adam_eps = 1e-08
adam_step = 100.0
num_param = 59
num_record = 11
num_view = 4
gauss_dev = 1024
shards = 128
cap = 4
slots = 512
slot_rows = 16
tile_dev = 2
list_len = 512
halves = 2


def project(gauss, camera, center_y):
    rotation = [[camera[3 * i + j] for j in range(3)] for i in range(3)]
    offset = [camera[9 + i] for i in range(3)]
    centre = [gauss[i] for i in range(3)]
    viewed = [sum((rotation[i][j] * centre[j] for j in range(3))) + offset[i] for i in range(3)]
    inverse = 1.0 / viewed[2]
    screen_x = focal_len * viewed[0] * inverse + center_x
    screen_y = focal_len * viewed[1] * inverse + center_y
    scales = [jnp.exp(gauss[3 + i]) for i in range(3)]
    length = jnp.sqrt(
        gauss[6] * gauss[6] + gauss[7] * gauss[7] + gauss[8] * gauss[8] + gauss[9] * gauss[9]
    )
    quat_w, quat_x, quat_y, quat_z = [gauss[6 + i] / length for i in range(4)]
    spin = [
        [
            1.0 - 2.0 * (quat_y * quat_y + quat_z * quat_z),
            2.0 * (quat_x * quat_y - quat_w * quat_z),
            2.0 * (quat_x * quat_z + quat_w * quat_y),
        ],
        [
            2.0 * (quat_x * quat_y + quat_w * quat_z),
            1.0 - 2.0 * (quat_x * quat_x + quat_z * quat_z),
            2.0 * (quat_y * quat_z - quat_w * quat_x),
        ],
        [
            2.0 * (quat_x * quat_z - quat_w * quat_y),
            2.0 * (quat_y * quat_z + quat_w * quat_x),
            1.0 - 2.0 * (quat_x * quat_x + quat_y * quat_y),
        ],
    ]
    factor = [[spin[i][j] * scales[j] for j in range(3)] for i in range(3)]
    sigma = [
        [sum((factor[i][j] * factor[k][j] for j in range(3))) for k in range(3)] for i in range(3)
    ]
    near = focal_len * inverse
    lean_x = -focal_len * viewed[0] * inverse * inverse
    lean_y = -focal_len * viewed[1] * inverse * inverse
    jacob = [
        [near * rotation[0][j] + lean_x * rotation[2][j] for j in range(3)],
        [near * rotation[1][j] + lean_y * rotation[2][j] for j in range(3)],
    ]
    halfway = [
        [sum((jacob[a][i] * sigma[i][k] for i in range(3))) for k in range(3)] for a in range(2)
    ]
    upper = sum((halfway[0][k] * jacob[0][k] for k in range(3))) + 0.3
    middle = sum((halfway[0][k] * jacob[1][k] for k in range(3)))
    lower = sum((halfway[1][k] * jacob[1][k] for k in range(3))) + 0.3
    determinant = upper * lower - middle * middle
    conic_a = lower / determinant
    conic_b = -middle / determinant
    conic_c = upper / determinant
    opacity = jax.nn.sigmoid(gauss[10])
    camera_pos = [-sum((rotation[i][j] * offset[i] for i in range(3))) for j in range(3)]
    toward = [centre[j] - camera_pos[j] for j in range(3)]
    reach = jnp.sqrt(toward[0] * toward[0] + toward[1] * toward[1] + toward[2] * toward[2])
    unit_x = toward[0] / reach
    unit_y = toward[1] / reach
    unit_z = toward[2] / reach
    square_x = unit_x * unit_x
    square_y = unit_y * unit_y
    square_z = unit_z * unit_z
    basis = [
        harm_zero + 0.0 * unit_x,
        -harm_one * unit_y,
        harm_one * unit_z,
        -harm_one * unit_x,
        harm_two[0] * unit_x * unit_y,
        harm_two[1] * unit_y * unit_z,
        harm_two[2] * (2.0 * square_z - square_x - square_y),
        harm_two[3] * unit_x * unit_z,
        harm_two[4] * (square_x - square_y),
        harm_three[0] * unit_y * (3.0 * square_x - square_y),
        harm_three[1] * unit_x * unit_y * unit_z,
        harm_three[2] * unit_y * (4.0 * square_z - square_x - square_y),
        harm_three[3] * unit_z * (2.0 * square_z - 3.0 * square_x - 3.0 * square_y),
        harm_three[4] * unit_x * (4.0 * square_z - square_x - square_y),
        harm_three[5] * unit_z * (square_x - square_y),
        harm_three[6] * unit_x * (square_x - 3.0 * square_y),
    ]
    colors = [0.5 + sum((basis[k] * gauss[11 + 16 * c + k] for k in range(16))) for c in range(3)]
    return [
        screen_x,
        screen_y,
        conic_a,
        conic_b,
        conic_c,
        opacity,
        colors[0],
        colors[1],
        colors[2],
        viewed[2],
        inverse,
    ]


def split_three(values):
    high = values.astype(jnp.bfloat16)
    left = values - high.astype(jnp.float32)
    middle = left.astype(jnp.bfloat16)
    low = (left - middle.astype(jnp.float32)).astype(jnp.bfloat16)
    return high, middle, low


def split_two(values):
    high = values.astype(jnp.bfloat16)
    return high, (values - high.astype(jnp.float32)).astype(jnp.bfloat16)


def contract(left, right, left_dim, right_dim):
    return lax.dot_general(
        left,
        right,
        (((left_dim,), (right_dim,)), ((), ())),
        preferred_element_type=jnp.float32,
    )


def as_mask(condition):
    return jnp.where(condition, jnp.bfloat16(1.0), jnp.bfloat16(0.0))


def short(values):
    return values.astype(jnp.int16)


def write_order(lists, places, key_out, before_out):
    order = jnp.concatenate([lists[0, t : t + 1] for t in range(tile_dev)], axis=1)
    total = tile_dev * list_len
    source = lax.broadcasted_iota(jnp.int32, (shards, total), 0)
    found = as_mask(short(source) == short(order >> 2))
    number = lax.broadcasted_iota(jnp.int32, (8, total), 1) + 1
    row = lax.broadcasted_iota(jnp.int32, (8, total), 0)
    digits = jnp.where(row < 4, number >> 8, number & 255)
    digits = jnp.where((order & 3) == (row & 3), digits, 0).astype(jnp.float32)
    keys = contract(digits.astype(jnp.bfloat16), found, 1, 1)
    keys = 256.0 * keys[0:4] + keys[4:8]
    key = jnp.concatenate([keys[c : c + 1] for c in range(cap)], axis=1)
    key_all = jnp.broadcast_to(key, (8, slots))
    key_col = key_all.T[:, 0:1]
    floor = jnp.where(key > float(list_len), float(list_len), 0.0)
    second = key > float(list_len)
    corner_x = [((places[0, t] & 63) * 16).astype(jnp.float32) + 8.0 for t in range(tile_dev)]
    corner_y = [((places[0, t] >> 6) * 16).astype(jnp.float32) + 8.0 for t in range(tile_dev)]
    key_out[0:1] = key
    key_out[1:2] = jnp.where(second, corner_x[1], corner_x[0])
    key_out[2:3] = jnp.where(second, corner_y[1], corner_y[0])
    key_col, key, floor = [short(part.astype(jnp.int32)) for part in (key_col, key, floor)]
    before_out[...] = as_mask((key_col < key) & (key_col > floor))


def send_kernel(
    center_y, params_in, lists_in, route_in, count_in, camera_in, places_in,
    visible_in, out, key_out, before_out, rows_out, cams_out, visible_out,
    params, lists, route, count, camera, places, turned, sems
):
    sources = (lists_in, route_in, camera_in, params_in, count_in, places_in, visible_in)
    kept = (lists, route, camera, params, count, places, visible_out)
    copies = [
        pltpu.make_async_copy(source, held, sems.at[i])
        for i, (source, held) in enumerate(zip(sources, kept))
    ]
    for copy in copies:
        copy.start()
    copies[0].wait()
    copies[5].wait()
    write_order(lists, places, key_out, before_out)
    copies[1].wait()
    chosen = route[0]
    sub = lax.broadcasted_iota(jnp.int32, (128, slots), 0)
    choose = as_mask(short(sub) == short(chosen & 127))
    copies[2].wait()
    cam = [camera[0, i] for i in range(12)]
    for i in range(16):
        cams_out[i : i + 1] = jnp.full((1, shards), cam[i] if i < 12 else 0.0, jnp.float32)
    copies[3].wait()
    rows = params[...].reshape(num_param, 8, 128)
    rows_out[...] = rows
    records = project([rows[i] for i in range(num_param)], cam, center_y)
    table = jnp.concatenate(split_three(jnp.concatenate(records, axis=0)), axis=0)
    picked = contract(table, choose, 1, 0)
    size = 8 * num_record
    picked = picked[0:size] + (picked[size : 2 * size] + picked[2 * size :])
    high = lax.broadcasted_iota(jnp.int32, (8, slots), 0) == (chosen >> 7)
    sent = [
        jnp.sum(jnp.where(high, picked[8 * r : 8 * r + 8], 0.0), axis=0, keepdims=True)
        for r in range(num_record)
    ]
    sent.append((chosen + 1).astype(jnp.float32))
    sent.append(jnp.zeros((slot_rows - num_record - 1, slots), jnp.float32))
    sent = jnp.concatenate(sent, axis=0)
    turned[:, 0:slot_rows] = sent.T
    parts = [turned[pl.ds(c, shards, stride=cap), :][:, 0:slot_rows] for c in range(cap)]
    width = cap * slot_rows
    spread = jnp.concatenate(parts + [jnp.zeros((shards, 128 - width), jnp.float32)], axis=1)
    copies[4].wait()
    used = jnp.broadcast_to(count[0], (8, shards)).T[:, 0:1]
    lane = lax.broadcasted_iota(jnp.int32, (shards, 128), 1)
    out[...] = jnp.where((lane >> 4) < used, spread, 0.0)
    copies[6].wait()


def tile_kernel(arrived, keys, before_in, target, cams, image_out, out, image, sem):
    turned = arrived[...].T
    rec = jnp.concatenate([turned[c * slot_rows : (c + 1) * slot_rows] for c in range(cap)], axis=1)
    key = keys[0:1]
    second = key > float(list_len)
    before = before_in[...]
    at_x = rec[0:1] - keys[1:2]
    at_y = rec[1:2] - keys[2:3]
    con_a, con_b, con_c = rec[2:3], rec[3:4], rec[4:5]
    half_a, half_c = -0.5 * con_a, -0.5 * con_c
    opacity = jnp.where(key > 0.0, rec[5:6], 0.0)
    feats = rec[6:11]
    gap = jnp.zeros((3, slots), jnp.float32)
    feats = jnp.concatenate(
        [jnp.where(second, 0.0, feats), gap, jnp.where(second, feats, 0.0), gap], axis=0
    )
    f_hi, f_lo, f_last = split_three(feats)
    f_both = jnp.concatenate([f_hi, f_lo], axis=0)
    f_six = jnp.concatenate([f_hi, f_lo, f_hi, f_lo, f_last, f_hi], axis=0)
    size = 256 // halves
    rows = range(halves)
    seat = lax.broadcasted_iota(jnp.int32, (8, size), 1)
    row = lax.broadcasted_iota(jnp.int32, (8, size), 0)
    seat_x = (seat & 15).astype(jnp.float32) - 7.5
    gap = jnp.zeros((3, size), jnp.float32)

    side = lax.broadcasted_iota(jnp.int32, (16, 1), 0).astype(jnp.float32) - 7.5
    scale = 1.4426950408889634
    apart_x = side - at_x
    slope_x = (scale * half_a) * apart_x
    apart_y = side - at_y
    slope_y = (scale * con_b) * apart_y
    bend_y = (scale * half_c) * apart_y * apart_y

    def shade(i):
        power = [
            apart_x * (slope_x - slope_y[y : y + 1]) + bend_y[y : y + 1]
            for y in range(i * size // 16, (i + 1) * size // 16)
        ]
        alpha = opacity * jnp.exp2(jnp.concatenate(power, axis=0))
        keep = 1.0 - alpha
        return alpha, keep, jnp.concatenate(split_two(jnp.log(keep)), axis=0)

    def blend(i, alpha, logs):
        sums = contract(logs, before, 1, 0)
        through = jnp.exp(sums[0:size] + sums[size:])
        weight = alpha * through
        return weight, split_two(weight)

    def draw(i, w_hi, w_lo):
        drawn = contract(f_both, w_hi, 1, 1)
        drawn = drawn[0:16] + (drawn[16:32] + contract(f_hi, w_lo, 1, 1))
        parts = []
        for t in range(tile_dev):
            shown = drawn[8 * t : 8 * t + 5]
            spot = pl.ds(t * 256 + i * size, size)
            for ch in range(5):
                image[ch, :, spot] = shown[ch : ch + 1]
            wanted = jnp.concatenate([target[ch, :, spot] for ch in range(5)], axis=0)
            parts += [shown - wanted, gap]
        return split_three(jnp.concatenate(parts, axis=0))

    def score_of(g_hi, g_lo, g_last, weight):
        score = contract(
            jnp.concatenate([g_hi, g_hi, g_lo, g_lo, g_hi, g_last], axis=0), f_six, 0, 0
        )
        gain = weight * score
        return gain, jnp.concatenate(split_two(gain), axis=0)

    def pull_of(ratio, gain, tails):
        tail = contract(tails, before, 1, 1)
        tail = tail[0:size] + tail[size:]
        return jnp.concatenate(split_three(gain - ratio * tail), axis=0)

    def moments_of(i, pull):
        seat_y = (seat >> 4).astype(jnp.float32) + (i * size // 16 - 7.5)
        first = jnp.where((row == 1) | (row == 3) | (row == 4), seat_x, 1.0)
        first = jnp.where((row == 2) | (row == 5), seat_y, first)
        other = jnp.where(row == 3, seat_x, 1.0)
        other = jnp.where((row == 4) | (row == 5), seat_y, other)
        basis = (first * other).astype(jnp.bfloat16)
        return contract(jnp.concatenate([basis] * 3, axis=1), pull, 1, 0)

    def colors_of(g_hi, g_lo, g_last, w_hi, w_lo):
        color = contract(jnp.concatenate([g_hi, g_lo], axis=0), w_hi, 1, 0)
        return color[0:16] + (color[16:32] + contract(g_hi, w_lo, 1, 0))

    shaded = [shade(i) for i in rows]
    blended = [blend(i, shaded[i][0], shaded[i][2]) for i in rows]
    diffs = [draw(i, *blended[i][1]) for i in rows]
    shown = pltpu.make_async_copy(image, image_out, sem)
    shown.start()
    scores = [score_of(*diffs[i], blended[i][0]) for i in rows]
    color = sum(colors_of(*diffs[i], *blended[i][1]) for i in rows)
    pulls = [
        pull_of(shaded[i][0] / shaded[i][1], *scores[i]) for i in rows
    ]
    moments = sum(moments_of(i, pulls[i]) for i in rows)
    m_0, m_x, m_y, m_xx, m_xy, m_yy = [moments[i : i + 1] for i in range(6)]
    d_x = m_x - at_x * m_0
    d_y = m_y - at_y * m_0
    d_xx = m_xx - at_x * (m_x + d_x)
    d_xy = m_xy - at_x * m_y - at_y * d_x
    d_yy = m_yy - at_y * (m_y + d_y)
    color = jnp.where(second, color[8:13], color[0:5])
    pulled = jnp.concatenate(
        [
            con_a * d_x + con_b * d_y,
            con_b * d_x + con_c * d_y,
            -0.5 * d_xx,
            -d_xy,
            -0.5 * d_yy,
            jnp.where(opacity > 0.0, m_0 / jnp.where(opacity > 0.0, opacity, 1.0), 0.0),
            color,
            rec[11:12],
        ],
        axis=0,
    )
    stacked = []
    for c in range(cap):
        stacked.append(pulled[:, c * shards : (c + 1) * shards])
        stacked.append(cams[4 * c : 4 * c + 4])
    stacked.append(jnp.zeros((128 - cap * slot_rows, shards), jnp.float32))
    block = jnp.concatenate(stacked, axis=0).T
    out[...] = block
    shown.wait()


def share_kernel(returned, out):
    block = returned[...].T[0 : cap * slot_rows]
    for w in range(num_view):
        out[w] = block


def update_kernel(center_y, grads, rows, params, adam_m, adam_v, visible, new_p, new_m, new_v):
    turned = [grads[w] for w in range(num_view)]
    slot = [turned[w][c * slot_rows : (c + 1) * slot_rows] for w in range(num_view) for c in range(cap)]
    slot = jnp.concatenate(slot, axis=1)
    total = num_view * slots
    number = slot[num_record : num_record + 1].astype(jnp.int32) - 1
    viewer = (lax.broadcasted_iota(jnp.int32, (1, total), 1) >> 9).astype(jnp.float32) + 1.0
    high = lax.broadcasted_iota(jnp.int32, (8, total), 0) == (number >> 7)
    place = as_mask(
        short(lax.broadcasted_iota(jnp.int32, (128, total), 0)) == short(number & 127)
    )
    coarse = slot.astype(jnp.bfloat16).astype(jnp.float32)
    fine = slot - coarse
    spread = [jnp.where(high, coarse[r : r + 1], 0.0) for r in range(num_record)]
    spread.append(jnp.where(high, viewer, 0.0))
    spread += [jnp.where(high, fine[r : r + 1], 0.0) for r in range(num_record)]
    placed = contract(jnp.concatenate(spread, axis=0).astype(jnp.bfloat16), place, 1, 1)
    size = 8 * num_record
    seen = placed[size : size + 8]
    placed = placed[0:size] + placed[size + 8 :]
    pulled = [placed[8 * r : 8 * r + 8] for r in range(num_record)]
    cam = []
    for i in range(12):
        spot = i // 4 * slot_rows + 12 + i % 4
        value = jnp.broadcast_to(turned[0][spot : spot + 1], (8, 128))
        for w in range(1, num_view):
            value = jnp.where(seen == w + 1.0, turned[w][spot : spot + 1], value)
        cam.append(value)
    _, pull = jax.vjp(
        lambda *gauss: project(gauss, cam, center_y), *[rows[i] for i in range(num_param)]
    )
    grad = jnp.stack(pull(pulled)).reshape(num_param, gauss_dev)
    keep = jnp.where(visible[...].reshape(1, gauss_dev) > 0, 1.0, 0.0)
    rate_one = (1.0 - beta_one) * keep
    rate_two = (1.0 - beta_two) * keep
    rate = (learn_rate / (1.0 - beta_one**adam_step)) * keep
    old, old_m, old_v = params[...], adam_m[...], adam_v[...]
    moment_one = old_m + rate_one * (grad - old_m)
    moment_two = old_v + rate_two * (grad * grad - old_v)
    second_hat = moment_two * (1.0 / (1.0 - beta_two**adam_step))
    new_p[...] = old - rate * moment_one / (jnp.sqrt(second_hat) + adam_eps)
    new_m[...] = moment_one
    new_v[...] = moment_two


def shaped(*dims):
    return jax.ShapeDtypeStruct(dims, jnp.float32)


def near(array):
    return pltpu.with_memory_space_constraint(array, pltpu.VMEM)


vector = pl.BlockSpec(memory_space=pltpu.VMEM)
scalar = pl.BlockSpec(memory_space=pltpu.SMEM)


def send_call(params, tile_lists, send_index, send_count, cameras, tile_pos, visible):
    return pl.pallas_call(
        functools.partial(send_kernel, 8.0 * (tile_dev * shards) / 64.0),
        out_shape=(
            pltpu.VMEM((shards, 128), jnp.float32),
            pltpu.VMEM((8, slots), jnp.float32),
            pltpu.VMEM((slots, slots), jnp.bfloat16),
            pltpu.VMEM((num_param, 8, 128), jnp.float32),
            pltpu.VMEM((16, shards), jnp.float32),
            pltpu.VMEM((8, 128), jnp.int32),
        ),
        in_specs=[pl.BlockSpec(memory_space=pl.ANY)] * 7,
        scratch_shapes=[
            pltpu.VMEM((num_param, gauss_dev), jnp.float32),
            pltpu.VMEM((1, tile_dev, list_len), jnp.int32),
            pltpu.VMEM((1, 1, slots), jnp.int32),
            pltpu.VMEM((1, 1, shards), jnp.int32),
            pltpu.SMEM((1, 12), jnp.float32),
            pltpu.SMEM((1, tile_dev), jnp.int32),
            pltpu.VMEM((slots, 128), jnp.float32),
            pltpu.SemaphoreType.DMA((7,)),
        ],
        name="send",
    )(params, tile_lists, send_index, send_count, cameras, tile_pos, visible)


def tile_call(arrived, keys, before, target, cams):
    return pl.pallas_call(
        tile_kernel,
        out_shape=(
            shaped(5, 1, tile_dev * 256),
            pltpu.VMEM((shards, 128), jnp.float32),
        ),
        in_specs=[vector] * 5,
        out_specs=[pl.BlockSpec(memory_space=pl.ANY), vector],
        scratch_shapes=[
            pltpu.VMEM((5, 1, tile_dev * 256), jnp.float32),
            pltpu.SemaphoreType.DMA,
        ],
        name="tiles",
    )(near(arrived), near(keys), near(before), near(target), near(cams))


def share_call(returned):
    return pl.pallas_call(
        share_kernel,
        out_shape=pltpu.VMEM((num_view, cap * slot_rows, shards), jnp.float32),
        in_specs=[vector],
        name="share",
    )(near(returned))


def update_call(grads, rows, params, adam_m, adam_v, visible):
    return pl.pallas_call(
        functools.partial(update_kernel, 8.0 * (tile_dev * shards) / 64.0),
        out_shape=(shaped(num_param, gauss_dev),) * 3,
        in_specs=[vector] * 6,
        name="update",
    )(near(grads), near(rows), near(params), near(adam_m), near(adam_v), near(visible))


def body(
    params, adam_m, adam_v, visible, cameras, send_index, send_count, tile_lists, tile_pos, target
):
    sending, keys, before, rows, cams, shown = send_call(
        params, tile_lists, send_index, send_count, cameras, tile_pos, visible.reshape(8, 128)
    )
    arrived = lax.all_to_all(sending, "space", split_axis=0, concat_axis=0, tiled=True)
    wanted = jnp.transpose(target, (1, 0, 2))
    image, pulled = tile_call(arrived, keys, before, wanted, cams)
    image = jnp.transpose(image, (1, 0, 2))
    pulled = lax.all_to_all(pulled, "space", split_axis=0, concat_axis=0, tiled=True)
    grads = lax.all_to_all(share_call(pulled), "view", split_axis=0, concat_axis=0, tiled=True)
    new_params, new_m, new_v = update_call(grads, rows, params, adam_m, adam_v, shown)
    return (image, new_params, new_m, new_v)


def solution(mesh):
    placed = (
        P(None, "space"),
        P(None, "space"),
        P(None, "space"),
        P("space"),
        P("view", None),
        P("view", "space", None),
        P("view", "space", None),
        P("view", "space", None),
        P("view", "space"),
        P("view", None, "space"),
    )
    return jax.shard_map(
        body,
        mesh=mesh,
        in_specs=placed,
        out_specs=(P("view", None, "space"), P(None, "space"), P(None, "space"), P(None, "space")),
        check_vma=False,
    )
```

```python
import functools

import jax
import jax.numpy as jnp
from jax import lax
from jax.experimental import pallas as pl
from jax.experimental.pallas import tpu as pltpu
from jax.sharding import PartitionSpec as P

focal_len = 1000.0
center_x = 512.0
harm_zero = 0.28209479177387814
harm_one = 0.4886025119029199
harm_two = (
    1.0925484305920792,
    -1.0925484305920792,
    0.31539156525252005,
    -1.0925484305920792,
    0.5462742152960396,
)
harm_three = (
    -0.5900435899266435,
    2.890611442640554,
    -0.4570457994644658,
    0.3731763325901154,
    -0.4570457994644658,
    1.445305721320277,
    -0.5900435899266435,
)
beta_one = 0.9
beta_two = 0.99
learn_rate = 0.05
adam_eps = 1e-08
adam_step = 100.0
num_param = 59
num_record = 11
num_view = 4
gauss_dev = 1024
shards = 128
cap = 4
slots = 512
slot_rows = 16
tile_dev = 2
list_len = 512
halves = 2


def project(gauss, camera, center_y):
    rotation = [[camera[3 * i + j] for j in range(3)] for i in range(3)]
    offset = [camera[9 + i] for i in range(3)]
    centre = [gauss[i] for i in range(3)]
    viewed = [sum((rotation[i][j] * centre[j] for j in range(3))) + offset[i] for i in range(3)]
    inverse = 1.0 / viewed[2]
    screen_x = focal_len * viewed[0] * inverse + center_x
    screen_y = focal_len * viewed[1] * inverse + center_y
    scales = [jnp.exp(gauss[3 + i]) for i in range(3)]
    length = jnp.sqrt(
        gauss[6] * gauss[6] + gauss[7] * gauss[7] + gauss[8] * gauss[8] + gauss[9] * gauss[9]
    )
    quat_w, quat_x, quat_y, quat_z = [gauss[6 + i] / length for i in range(4)]
    spin = [
        [
            1.0 - 2.0 * (quat_y * quat_y + quat_z * quat_z),
            2.0 * (quat_x * quat_y - quat_w * quat_z),
            2.0 * (quat_x * quat_z + quat_w * quat_y),
        ],
        [
            2.0 * (quat_x * quat_y + quat_w * quat_z),
            1.0 - 2.0 * (quat_x * quat_x + quat_z * quat_z),
            2.0 * (quat_y * quat_z - quat_w * quat_x),
        ],
        [
            2.0 * (quat_x * quat_z - quat_w * quat_y),
            2.0 * (quat_y * quat_z + quat_w * quat_x),
            1.0 - 2.0 * (quat_x * quat_x + quat_y * quat_y),
        ],
    ]
    factor = [[spin[i][j] * scales[j] for j in range(3)] for i in range(3)]
    sigma = [
        [sum((factor[i][j] * factor[k][j] for j in range(3))) for k in range(3)] for i in range(3)
    ]
    near = focal_len * inverse
    lean_x = -focal_len * viewed[0] * inverse * inverse
    lean_y = -focal_len * viewed[1] * inverse * inverse
    jacob = [
        [near * rotation[0][j] + lean_x * rotation[2][j] for j in range(3)],
        [near * rotation[1][j] + lean_y * rotation[2][j] for j in range(3)],
    ]
    halfway = [
        [sum((jacob[a][i] * sigma[i][k] for i in range(3))) for k in range(3)] for a in range(2)
    ]
    upper = sum((halfway[0][k] * jacob[0][k] for k in range(3))) + 0.3
    middle = sum((halfway[0][k] * jacob[1][k] for k in range(3)))
    lower = sum((halfway[1][k] * jacob[1][k] for k in range(3))) + 0.3
    determinant = upper * lower - middle * middle
    conic_a = lower / determinant
    conic_b = -middle / determinant
    conic_c = upper / determinant
    opacity = jax.nn.sigmoid(gauss[10])
    camera_pos = [-sum((rotation[i][j] * offset[i] for i in range(3))) for j in range(3)]
    toward = [centre[j] - camera_pos[j] for j in range(3)]
    reach = jnp.sqrt(toward[0] * toward[0] + toward[1] * toward[1] + toward[2] * toward[2])
    unit_x = toward[0] / reach
    unit_y = toward[1] / reach
    unit_z = toward[2] / reach
    square_x = unit_x * unit_x
    square_y = unit_y * unit_y
    square_z = unit_z * unit_z
    basis = [
        harm_zero + 0.0 * unit_x,
        -harm_one * unit_y,
        harm_one * unit_z,
        -harm_one * unit_x,
        harm_two[0] * unit_x * unit_y,
        harm_two[1] * unit_y * unit_z,
        harm_two[2] * (2.0 * square_z - square_x - square_y),
        harm_two[3] * unit_x * unit_z,
        harm_two[4] * (square_x - square_y),
        harm_three[0] * unit_y * (3.0 * square_x - square_y),
        harm_three[1] * unit_x * unit_y * unit_z,
        harm_three[2] * unit_y * (4.0 * square_z - square_x - square_y),
        harm_three[3] * unit_z * (2.0 * square_z - 3.0 * square_x - 3.0 * square_y),
        harm_three[4] * unit_x * (4.0 * square_z - square_x - square_y),
        harm_three[5] * unit_z * (square_x - square_y),
        harm_three[6] * unit_x * (square_x - 3.0 * square_y),
    ]
    colors = [0.5 + sum((basis[k] * gauss[11 + 16 * c + k] for k in range(16))) for c in range(3)]
    return [
        screen_x,
        screen_y,
        conic_a,
        conic_b,
        conic_c,
        opacity,
        colors[0],
        colors[1],
        colors[2],
        viewed[2],
        inverse,
    ]


def split_three(values):
    high = values.astype(jnp.bfloat16)
    left = values - high.astype(jnp.float32)
    middle = left.astype(jnp.bfloat16)
    low = (left - middle.astype(jnp.float32)).astype(jnp.bfloat16)
    return high, middle, low


def split_two(values):
    high = values.astype(jnp.bfloat16)
    return high, (values - high.astype(jnp.float32)).astype(jnp.bfloat16)


def contract(left, right, left_dim, right_dim):
    return lax.dot_general(
        left,
        right,
        (((left_dim,), (right_dim,)), ((), ())),
        preferred_element_type=jnp.float32,
    )


def as_mask(condition):
    return jnp.where(condition, jnp.bfloat16(1.0), jnp.bfloat16(0.0))


def short(values):
    return values.astype(jnp.int16)


def write_order(lists, places, key_out, before_out):
    order = jnp.concatenate([lists[0, t : t + 1] for t in range(tile_dev)], axis=1)
    total = tile_dev * list_len
    source = lax.broadcasted_iota(jnp.int32, (shards, total), 0)
    found = as_mask(short(source) == short(order >> 2))
    number = lax.broadcasted_iota(jnp.int32, (8, total), 1) + 1
    row = lax.broadcasted_iota(jnp.int32, (8, total), 0)
    digits = jnp.where(row < 4, number >> 8, number & 255)
    digits = jnp.where((order & 3) == (row & 3), digits, 0).astype(jnp.float32)
    keys = contract(digits.astype(jnp.bfloat16), found, 1, 1)
    keys = 256.0 * keys[0:4] + keys[4:8]
    key = jnp.concatenate([keys[c : c + 1] for c in range(cap)], axis=1)
    key_all = jnp.broadcast_to(key, (8, slots))
    key_col = key_all.T[:, 0:1]
    floor = jnp.where(key > float(list_len), float(list_len), 0.0)
    second = key > float(list_len)
    corner_x = [((places[0, t] & 63) * 16).astype(jnp.float32) + 8.0 for t in range(tile_dev)]
    corner_y = [((places[0, t] >> 6) * 16).astype(jnp.float32) + 8.0 for t in range(tile_dev)]
    key_out[0:1] = key
    key_out[1:2] = jnp.where(second, corner_x[1], corner_x[0])
    key_out[2:3] = jnp.where(second, corner_y[1], corner_y[0])
    key_col, key, floor = [short(part.astype(jnp.int32)) for part in (key_col, key, floor)]
    before_out[...] = as_mask((key_col < key) & (key_col > floor))


def send_kernel(
    center_y, params_in, lists_in, route_in, count_in, camera_in, places_in,
    visible_in, out, key_out, before_out, rows_out, cams_out, visible_out,
    params, lists, route, count, camera, places, turned, sems
):
    sources = (lists_in, route_in, camera_in, params_in, count_in, places_in, visible_in)
    kept = (lists, route, camera, params, count, places, visible_out)
    copies = [
        pltpu.make_async_copy(source, held, sems.at[i])
        for i, (source, held) in enumerate(zip(sources, kept))
    ]
    for copy in copies:
        copy.start()
    for copy in copies[:6]:
        copy.wait()
    write_order(lists, places, key_out, before_out)
    chosen = route[0]
    sub = lax.broadcasted_iota(jnp.int32, (128, slots), 0)
    choose = as_mask(short(sub) == short(chosen & 127))
    cam = [camera[0, i] for i in range(12)]
    for i in range(16):
        cams_out[i : i + 1] = jnp.full((1, shards), cam[i] if i < 12 else 0.0, jnp.float32)
    rows = params[...].reshape(num_param, 8, 128)
    rows_out[...] = rows
    records = project([rows[i] for i in range(num_param)], cam, center_y)
    table = jnp.concatenate(split_three(jnp.concatenate(records, axis=0)), axis=0)
    picked = contract(table, choose, 1, 0)
    size = 8 * num_record
    picked = picked[0:size] + (picked[size : 2 * size] + picked[2 * size :])
    high = lax.broadcasted_iota(jnp.int32, (8, slots), 0) == (chosen >> 7)
    sent = [
        jnp.sum(jnp.where(high, picked[8 * r : 8 * r + 8], 0.0), axis=0, keepdims=True)
        for r in range(num_record)
    ]
    sent.append((chosen + 1).astype(jnp.float32))
    sent.append(jnp.zeros((slot_rows - num_record - 1, slots), jnp.float32))
    sent = jnp.concatenate(sent, axis=0)
    turned[:, 0:slot_rows] = sent.T
    parts = [turned[pl.ds(c, shards, stride=cap), :][:, 0:slot_rows] for c in range(cap)]
    width = cap * slot_rows
    spread = jnp.concatenate(parts + [jnp.zeros((shards, 128 - width), jnp.float32)], axis=1)
    used = jnp.broadcast_to(count[0], (8, shards)).T[:, 0:1]
    lane = lax.broadcasted_iota(jnp.int32, (shards, 128), 1)
    out[...] = jnp.where((lane >> 4) < used, spread, 0.0)
    copies[6].wait()


def tile_kernel(arrived, keys, before_in, target, cams, image_out, out, image, sem):
    turned = arrived[...].T
    rec = jnp.concatenate([turned[c * slot_rows : (c + 1) * slot_rows] for c in range(cap)], axis=1)
    key = keys[0:1]
    second = key > float(list_len)
    before = before_in[...]
    at_x = rec[0:1] - keys[1:2]
    at_y = rec[1:2] - keys[2:3]
    con_a, con_b, con_c = rec[2:3], rec[3:4], rec[4:5]
    half_a, half_c = -0.5 * con_a, -0.5 * con_c
    opacity = jnp.where(key > 0.0, rec[5:6], 0.0)
    feats = rec[6:11]
    gap = jnp.zeros((3, slots), jnp.float32)
    feats = jnp.concatenate(
        [jnp.where(second, 0.0, feats), gap, jnp.where(second, feats, 0.0), gap], axis=0
    )
    f_hi, f_lo, f_last = split_three(feats)
    f_both = jnp.concatenate([f_hi, f_lo], axis=0)
    f_six = jnp.concatenate([f_hi, f_lo, f_hi, f_lo, f_last, f_hi], axis=0)
    size = 256 // halves
    rows = range(halves)
    seat = lax.broadcasted_iota(jnp.int32, (8, size), 1)
    row = lax.broadcasted_iota(jnp.int32, (8, size), 0)
    seat_x = (seat & 15).astype(jnp.float32) - 7.5
    gap = jnp.zeros((3, size), jnp.float32)

    side = lax.broadcasted_iota(jnp.int32, (16, 1), 0).astype(jnp.float32) - 7.5
    scale = 1.4426950408889634
    apart_x = side - at_x
    slope_x = (scale * half_a) * apart_x
    apart_y = side - at_y
    slope_y = (scale * con_b) * apart_y
    bend_y = (scale * half_c) * apart_y * apart_y

    def shade(i):
        power = [
            apart_x * (slope_x - slope_y[y : y + 1]) + bend_y[y : y + 1]
            for y in range(i * size // 16, (i + 1) * size // 16)
        ]
        alpha = opacity * jnp.exp2(jnp.concatenate(power, axis=0))
        keep = 1.0 - alpha
        return alpha, keep, jnp.concatenate(split_two(jnp.log(keep)), axis=0)

    def blend(i, alpha, logs):
        sums = contract(logs, before, 1, 0)
        through = jnp.exp(sums[0:size] + sums[size:])
        weight = alpha * through
        return weight, split_two(weight)

    def draw(i, w_hi, w_lo):
        drawn = contract(f_both, w_hi, 1, 1)
        drawn = drawn[0:16] + (drawn[16:32] + contract(f_hi, w_lo, 1, 1))
        parts = []
        for t in range(tile_dev):
            shown = drawn[8 * t : 8 * t + 5]
            spot = pl.ds(t * 256 + i * size, size)
            for ch in range(5):
                image[ch, :, spot] = shown[ch : ch + 1]
            wanted = jnp.concatenate([target[ch, :, spot] for ch in range(5)], axis=0)
            parts += [shown - wanted, gap]
        return split_three(jnp.concatenate(parts, axis=0))

    def score_of(g_hi, g_lo, g_last, weight):
        score = contract(
            jnp.concatenate([g_hi, g_hi, g_lo, g_lo, g_hi, g_last], axis=0), f_six, 0, 0
        )
        gain = weight * score
        return gain, jnp.concatenate(split_two(gain), axis=0)

    def pull_of(ratio, gain, tails):
        tail = contract(tails, before, 1, 1)
        tail = tail[0:size] + tail[size:]
        return jnp.concatenate(split_three(gain - ratio * tail), axis=0)

    def moments_of(i, pull):
        seat_y = (seat >> 4).astype(jnp.float32) + (i * size // 16 - 7.5)
        first = jnp.where((row == 1) | (row == 3) | (row == 4), seat_x, 1.0)
        first = jnp.where((row == 2) | (row == 5), seat_y, first)
        other = jnp.where(row == 3, seat_x, 1.0)
        other = jnp.where((row == 4) | (row == 5), seat_y, other)
        basis = (first * other).astype(jnp.bfloat16)
        return contract(jnp.concatenate([basis] * 3, axis=1), pull, 1, 0)

    def colors_of(g_hi, g_lo, g_last, w_hi, w_lo):
        color = contract(jnp.concatenate([g_hi, g_lo], axis=0), w_hi, 1, 0)
        return color[0:16] + (color[16:32] + contract(g_hi, w_lo, 1, 0))

    shaded = [shade(i) for i in rows]
    blended = [blend(i, shaded[i][0], shaded[i][2]) for i in rows]
    diffs = [draw(i, *blended[i][1]) for i in rows]
    shown = pltpu.make_async_copy(image, image_out, sem)
    shown.start()
    scores = [score_of(*diffs[i], blended[i][0]) for i in rows]
    color = sum(colors_of(*diffs[i], *blended[i][1]) for i in rows)
    pulls = [
        pull_of(shaded[i][0] / shaded[i][1], *scores[i]) for i in rows
    ]
    moments = sum(moments_of(i, pulls[i]) for i in rows)
    m_0, m_x, m_y, m_xx, m_xy, m_yy = [moments[i : i + 1] for i in range(6)]
    d_x = m_x - at_x * m_0
    d_y = m_y - at_y * m_0
    d_xx = m_xx - at_x * (m_x + d_x)
    d_xy = m_xy - at_x * m_y - at_y * d_x
    d_yy = m_yy - at_y * (m_y + d_y)
    color = jnp.where(second, color[8:13], color[0:5])
    pulled = jnp.concatenate(
        [
            con_a * d_x + con_b * d_y,
            con_b * d_x + con_c * d_y,
            -0.5 * d_xx,
            -d_xy,
            -0.5 * d_yy,
            jnp.where(opacity > 0.0, m_0 / jnp.where(opacity > 0.0, opacity, 1.0), 0.0),
            color,
            rec[11:12],
        ],
        axis=0,
    )
    stacked = []
    for c in range(cap):
        stacked.append(pulled[:, c * shards : (c + 1) * shards])
        stacked.append(cams[4 * c : 4 * c + 4])
    stacked.append(jnp.zeros((128 - cap * slot_rows, shards), jnp.float32))
    block = jnp.concatenate(stacked, axis=0).T
    out[...] = block
    shown.wait()


def share_kernel(returned, out):
    block = returned[...].T[0 : cap * slot_rows]
    for w in range(num_view):
        out[w] = block


def update_kernel(center_y, grads, rows, params, adam_m, adam_v, visible, new_p, new_m, new_v):
    turned = [grads[w] for w in range(num_view)]
    slot = [turned[w][c * slot_rows : (c + 1) * slot_rows] for w in range(num_view) for c in range(cap)]
    slot = jnp.concatenate(slot, axis=1)
    total = num_view * slots
    number = slot[num_record : num_record + 1].astype(jnp.int32) - 1
    viewer = (lax.broadcasted_iota(jnp.int32, (1, total), 1) >> 9).astype(jnp.float32) + 1.0
    high = lax.broadcasted_iota(jnp.int32, (8, total), 0) == (number >> 7)
    place = as_mask(
        short(lax.broadcasted_iota(jnp.int32, (128, total), 0)) == short(number & 127)
    )
    coarse = slot.astype(jnp.bfloat16).astype(jnp.float32)
    fine = slot - coarse
    spread = [jnp.where(high, coarse[r : r + 1], 0.0) for r in range(num_record)]
    spread.append(jnp.where(high, viewer, 0.0))
    spread += [jnp.where(high, fine[r : r + 1], 0.0) for r in range(num_record)]
    placed = contract(jnp.concatenate(spread, axis=0).astype(jnp.bfloat16), place, 1, 1)
    size = 8 * num_record
    seen = placed[size : size + 8]
    placed = placed[0:size] + placed[size + 8 :]
    pulled = [placed[8 * r : 8 * r + 8] for r in range(num_record)]
    cam = []
    for i in range(12):
        spot = i // 4 * slot_rows + 12 + i % 4
        value = jnp.broadcast_to(turned[0][spot : spot + 1], (8, 128))
        for w in range(1, num_view):
            value = jnp.where(seen == w + 1.0, turned[w][spot : spot + 1], value)
        cam.append(value)
    _, pull = jax.vjp(
        lambda *gauss: project(gauss, cam, center_y), *[rows[i] for i in range(num_param)]
    )
    grad = jnp.stack(pull(pulled)).reshape(num_param, gauss_dev)
    keep = jnp.where(visible[...].reshape(1, gauss_dev) > 0, 1.0, 0.0)
    rate_one = (1.0 - beta_one) * keep
    rate_two = (1.0 - beta_two) * keep
    rate = (learn_rate / (1.0 - beta_one**adam_step)) * keep
    old, old_m, old_v = params[...], adam_m[...], adam_v[...]
    moment_one = old_m + rate_one * (grad - old_m)
    moment_two = old_v + rate_two * (grad * grad - old_v)
    second_hat = moment_two * (1.0 / (1.0 - beta_two**adam_step))
    new_p[...] = old - rate * moment_one / (jnp.sqrt(second_hat) + adam_eps)
    new_m[...] = moment_one
    new_v[...] = moment_two


def shaped(*dims):
    return jax.ShapeDtypeStruct(dims, jnp.float32)


def near(array):
    return pltpu.with_memory_space_constraint(array, pltpu.VMEM)


vector = pl.BlockSpec(memory_space=pltpu.VMEM)
scalar = pl.BlockSpec(memory_space=pltpu.SMEM)


def send_call(params, tile_lists, send_index, send_count, cameras, tile_pos, visible):
    return pl.pallas_call(
        functools.partial(send_kernel, 8.0 * (tile_dev * shards) / 64.0),
        out_shape=(
            pltpu.VMEM((shards, 128), jnp.float32),
            pltpu.VMEM((8, slots), jnp.float32),
            pltpu.VMEM((slots, slots), jnp.bfloat16),
            pltpu.VMEM((num_param, 8, 128), jnp.float32),
            pltpu.VMEM((16, shards), jnp.float32),
            pltpu.VMEM((8, 128), jnp.int32),
        ),
        in_specs=[pl.BlockSpec(memory_space=pl.ANY)] * 7,
        scratch_shapes=[
            pltpu.VMEM((num_param, gauss_dev), jnp.float32),
            pltpu.VMEM((1, tile_dev, list_len), jnp.int32),
            pltpu.VMEM((1, 1, slots), jnp.int32),
            pltpu.VMEM((1, 1, shards), jnp.int32),
            pltpu.SMEM((1, 12), jnp.float32),
            pltpu.SMEM((1, tile_dev), jnp.int32),
            pltpu.VMEM((slots, 128), jnp.float32),
            pltpu.SemaphoreType.DMA((7,)),
        ],
        name="send",
    )(params, tile_lists, send_index, send_count, cameras, tile_pos, visible)


def tile_call(arrived, keys, before, target, cams):
    return pl.pallas_call(
        tile_kernel,
        out_shape=(
            shaped(5, 1, tile_dev * 256),
            pltpu.VMEM((shards, 128), jnp.float32),
        ),
        in_specs=[vector] * 5,
        out_specs=[pl.BlockSpec(memory_space=pl.ANY), vector],
        scratch_shapes=[
            pltpu.VMEM((5, 1, tile_dev * 256), jnp.float32),
            pltpu.SemaphoreType.DMA,
        ],
        name="tiles",
    )(near(arrived), near(keys), near(before), near(target), near(cams))


def share_call(returned):
    return pl.pallas_call(
        share_kernel,
        out_shape=pltpu.VMEM((num_view, cap * slot_rows, shards), jnp.float32),
        in_specs=[vector],
        name="share",
    )(near(returned))


def update_call(grads, rows, params, adam_m, adam_v, visible):
    return pl.pallas_call(
        functools.partial(update_kernel, 8.0 * (tile_dev * shards) / 64.0),
        out_shape=(shaped(num_param, gauss_dev),) * 3,
        in_specs=[vector] * 6,
        name="update",
    )(near(grads), near(rows), near(params), near(adam_m), near(adam_v), near(visible))


def body(
    params, adam_m, adam_v, visible, cameras, send_index, send_count, tile_lists, tile_pos, target
):
    sending, keys, before, rows, cams, shown = send_call(
        params, tile_lists, send_index, send_count, cameras, tile_pos, visible.reshape(8, 128)
    )
    arrived = lax.all_to_all(sending, "space", split_axis=0, concat_axis=0, tiled=True)
    wanted = jnp.transpose(target, (1, 0, 2))
    image, pulled = tile_call(arrived, keys, before, wanted, cams)
    image = jnp.transpose(image, (1, 0, 2))
    pulled = lax.all_to_all(pulled, "space", split_axis=0, concat_axis=0, tiled=True)
    grads = lax.all_to_all(share_call(pulled), "view", split_axis=0, concat_axis=0, tiled=True)
    new_params, new_m, new_v = update_call(grads, rows, params, adam_m, adam_v, shown)
    return (image, new_params, new_m, new_v)


def solution(mesh):
    placed = (
        P(None, "space"),
        P(None, "space"),
        P(None, "space"),
        P("space"),
        P("view", None),
        P("view", "space", None),
        P("view", "space", None),
        P("view", "space", None),
        P("view", "space"),
        P("view", None, "space"),
    )
    return jax.shard_map(
        body,
        mesh=mesh,
        in_specs=placed,
        out_specs=(P("view", None, "space"), P(None, "space"), P(None, "space"), P(None, "space")),
        check_vma=False,
    )
```
